256 devices in a mesh: row: 16 (over z_lo, y), col: 16 (over z_hi, x, core).
Axes of the slice: x: 4, y: 4, z: 8 (z_hi: 2, z_lo: 4; z = z_hi * 4 + z_lo), core: 2. Of those that a mesh axis runs over, the one named last changes fastest.
Arguments:
- features: bfloat16 [16384, 512], P(('row', 'col')), may hold values from -6 to 6
- w_first: bfloat16 [512, 512], replicated, may hold values from -0.25 to 0.25
- w_second: bfloat16 [512, 512], replicated, may hold values from -0.25 to 0.25
- block_index: int32 [16, 16, 64], P('row', 'col'), may hold values from 0 to 63, as said below
- block_count: int32 [16, 16], P('row', 'col'), may hold values from 0 to 16, as said below
- block_values: bfloat16 [16, 16, 64, 128, 128], P('row', 'col'), may hold values from -0.15625 to 0.15625
- cotangent: bfloat16 [16384, 512], P(('row', 'col')), may hold values from -0.046875 to 0.046875
Outputs:
- out_second: bfloat16 [16384, 512], P(('row', 'col'))
- grad_first: float32 [512, 512], replicated
- grad_second: float32 [512, 512], replicated
The draws below stay inside these ranges and needn't reach their ends.
Inputs may be any that keep to these rules, and one draw needn't show every extreme that they name: `block_index`: in each tile the 64 slots name every block position p = r * 8 + c (block row r, block column c of the tile) once, in some order; the first block_count slots are the tile's nonzero blocks and the others are unused. `block_count`: nonzero blocks of each tile; in every draw some tile has exactly 16.
All inputs are finite; a program needn't handle non-finite values.
Results may differ from the reference program's by a relative error of at most 0.0061.
Values may be sent and summed in bfloat16 or wider, within the bound.
A program may use at most 64 MiB of HBM per device.

```python
import jax
import jax.numpy as jnp
from jax import lax

WIDTH = 512
BLOCK = 128
ROW_TILES = 16
COL_TILES = 16
NODES = 16384
TILE_ROWS = 1024
TILE_COLS = 1024
BLK_ROWS = 8
BLK_COLS = 8
SLOTS = 64
MAX_BLOCKS = 16
N_ROW = 16
N_COL = 16


def tile_pattern(key):
    base = jax.random.fold_in(key, 4099)
    key_rows, key_cols, key_roll, key_full, key_order = jax.random.split(base, 5)
    brow_total = ROW_TILES * BLK_ROWS
    bcol_total = COL_TILES * BLK_COLS
    level_rows = jax.random.randint(key_rows, (brow_total,), 1, 5, dtype=jnp.int32)
    level_cols = jax.random.randint(key_cols, (bcol_total,), 1, 5, dtype=jnp.int32)
    roll = jax.random.randint(key_roll, (brow_total, bcol_total), 0, 64, dtype=jnp.int32)
    present = (roll < level_rows[:, None] * level_cols[None, :]).astype(jnp.int32)
    present = present.reshape(ROW_TILES, BLK_ROWS, COL_TILES, BLK_COLS)
    present = present.transpose(0, 2, 1, 3).reshape(ROW_TILES, COL_TILES, SLOTS)
    chosen = jax.random.randint(key_full, (), 0, ROW_TILES * COL_TILES, dtype=jnp.int32)
    tile_ident = jnp.arange(ROW_TILES, dtype=jnp.int32)[:, None] * COL_TILES + jnp.arange(COL_TILES, dtype=jnp.int32)[None, :]
    present = jnp.where((tile_ident == chosen)[:, :, None], 1, present)
    shuffle = jax.random.randint(key_order, (ROW_TILES, COL_TILES, SLOTS), 0, SLOTS, dtype=jnp.int32)
    position = jnp.arange(SLOTS, dtype=jnp.int32)
    score = (1 - present) * (SLOTS * SLOTS) + shuffle * SLOTS + position[None, None, :]
    order = jnp.argsort(score, axis=-1, stable=True).astype(jnp.int32)
    totals = jnp.minimum(jnp.sum(present, axis=-1), MAX_BLOCKS).astype(jnp.int32)
    return (order, totals)


def draw_block_index(key, part):
    return tile_pattern(key)[0]


def draw_block_count(key, part):
    return tile_pattern(key)[1]


def block_scale(own_key, shape, cuts, least, high):
    gain = 1.0
    for dim, blocks in cuts:
        steps = jax.random.uniform(jax.random.fold_in(jax.random.fold_in(own_key, 6), dim), (blocks,), jnp.float32, least / len(cuts), high / len(cuts))
        gain = gain * jnp.repeat(jnp.exp(steps), shape[dim] // blocks).reshape((-1,) + (1,) * (len(shape) - 1 - dim))
    return gain


def centred(own_key, dims, scale, limit, cuts=(), held_as=jnp.bfloat16):
    array = scale * jax.random.normal(own_key, dims, jnp.float32)
    if cuts:
        array = array * block_scale(own_key, dims, cuts, -0.22, 0.18)
    return jnp.clip(array, -limit, limit).astype(held_as)


def setup_inputs(seed: int = 0) -> dict:
    key_list = jax.random.split(jax.random.key(seed), 8)
    return {
        "features": centred(key_list[0], (NODES, WIDTH), 1.0, 6.0, ((0, 256),)),
        "w_first": centred(key_list[1], (WIDTH, WIDTH), WIDTH ** -0.5, 0.25),
        "w_second": centred(key_list[2], (WIDTH, WIDTH), WIDTH ** -0.5, 0.25),
        "block_index": draw_block_index(jax.random.fold_in(key_list[7], 71), 0),
        "block_count": draw_block_count(jax.random.fold_in(key_list[7], 71), 0),
        "block_values": centred(key_list[5], (ROW_TILES, COL_TILES, SLOTS, BLOCK, BLOCK), (max(NODES // 10, BLOCK)) ** -0.5, 0.15625, ((0, 16), (1, 16))),
        "cotangent": centred(key_list[6], (NODES, WIDTH), NODES ** -0.5, 0.046875, ((0, 256),)),
    }


def activate(v):
    return jax.nn.gelu(v, approximate=True)

def tile_term(tile_values, slot_index, slot_count, panel_part, flip):
    is_live = jnp.arange(SLOTS, dtype=jnp.int32) < slot_count
    block_row = slot_index // BLK_COLS
    block_col = slot_index % BLK_COLS
    values_wide = tile_values.astype(jnp.float32)
    feat_width = panel_part.shape[1]
    if flip:
        picked = panel_part.reshape(BLK_ROWS, BLOCK, feat_width)[block_row].astype(jnp.float32)
        product = jnp.einsum('sab,saf->sbf', values_wide, picked, precision=lax.Precision.HIGHEST)
        target = block_col
        out_blocks = BLK_COLS
    else:
        picked = panel_part.reshape(BLK_COLS, BLOCK, feat_width)[block_col].astype(jnp.float32)
        product = jnp.einsum('sab,sbf->saf', values_wide, picked, precision=lax.Precision.HIGHEST)
        target = block_row
        out_blocks = BLK_ROWS
    targets = jnp.arange(out_blocks, dtype=jnp.int32)
    onehot = ((target[None, :] == targets[:, None]) & is_live[None, :]).astype(jnp.float32)
    term = jnp.einsum('os,saf->oaf', onehot, product, precision=lax.Precision.HIGHEST)
    return term.reshape(out_blocks * BLOCK, feat_width)

def aggregate(block_values, block_index, block_count, panel, flip):
    feat_width = panel.shape[1]
    if flip:
        outer_count, inner_count, out_rows = (N_COL, N_ROW, TILE_COLS)
    else:
        outer_count, inner_count, out_rows = (N_ROW, N_COL, TILE_ROWS)

    def band(outer_no):

        def add(total, inner_no):
            if flip:
                row_no, col_no = (inner_no, outer_no)
                part = lax.dynamic_slice_in_dim(panel, (row_no * TILE_ROWS).astype(jnp.int32), TILE_ROWS, 0)
            else:
                row_no, col_no = (outer_no, inner_no)
                part = lax.dynamic_slice_in_dim(panel, (col_no * TILE_COLS).astype(jnp.int32), TILE_COLS, 0)
            term = tile_term(block_values[row_no, col_no], block_index[row_no, col_no], block_count[row_no, col_no], part, flip)
            return (total + term, None)
        total, _ = lax.scan(add, jnp.zeros((out_rows, feat_width), jnp.float32), jnp.arange(inner_count, dtype=jnp.int32))
        return total
    bands = lax.map(band, jnp.arange(outer_count, dtype=jnp.int32))
    return bands.reshape(NODES, feat_width)

def reference(features, w_first, w_second, block_index, block_count, block_values, cotangent):
    first_linear = jnp.dot(features, w_first, preferred_element_type=jnp.float32).astype(jnp.bfloat16)
    first_sum = aggregate(block_values, block_index, block_count, first_linear, True)
    first_value, act_back = jax.vjp(activate, first_sum)
    first_active = first_value.astype(jnp.bfloat16)
    second_linear = jnp.dot(first_active, w_second, preferred_element_type=jnp.float32).astype(jnp.bfloat16)
    out_second = aggregate(block_values, block_index, block_count, second_linear, False).astype(jnp.bfloat16)
    back_second = aggregate(block_values, block_index, block_count, cotangent, True).astype(jnp.bfloat16)
    grad_second = jnp.dot(first_active.T, back_second, preferred_element_type=jnp.float32)
    back_act = jnp.dot(back_second, w_second.T, preferred_element_type=jnp.float32)
    back_first = act_back(back_act)[0].astype(jnp.bfloat16)
    back_linear = aggregate(block_values, block_index, block_count, back_first, False).astype(jnp.bfloat16)
    grad_first = jnp.dot(features.T, back_linear, preferred_element_type=jnp.float32)
    return (out_second, grad_first, grad_second)
```

```python
import jax
import jax.numpy as jnp
from jax import lax
from jax.experimental import pallas as pl
from jax.experimental.pallas import tpu as pltpu
from jax.sharding import PartitionSpec as P

MESH = pl.DeviceIdType.MESH
BF = jnp.bfloat16
F32 = jnp.float32
ROWS = 64
WIDTH = 512
LIVE = 16
GELU_A = 0.7978845608
GELU_B = 0.044715


def dot(a, b):
    return jnp.dot(a, b, preferred_element_type=F32)


def kernel(
    table, feat, cot, w1_hbm, w2_hbm, vals_hbm, out_hbm, grad_hbm,
    X, PT, RY, Q, RZ, Y, PO, RK, Q2, RX, Q3, RH, S, ST, V, VT, W1, W2,
    GS, GB, TG, GT, RGX, GY, RGY, GZ, RGZ, FZ, FG, ACT, OUT, KEEP,
    ssem, rsX, rsRY, rsRZ, rsY, rsRK, rsRX, rsRH, rsGB, rsRGX, rsRGY, rsRGZ, rsFZ, rsFY, rsFX, rsFK, lsem,
):
    r = lax.axis_index("row")
    c = lax.axis_index("col")
    z, y = r // 4, r % 4
    h, x, k = c // 8, (c // 2) % 4, c % 2
    q = h * 4 + z
    nh, nk = 1 - h, 1 - k

    def dev(z=z, y=y, h=h, x=x, k=k):
        return (z * 4 + y, h * 8 + x * 2 + k)

    xs = [(x + d) % 4 for d in (1, 3, 2)]
    ys = [(y + d) % 4 for d in (1, 3, 2)]
    zs = [(z + d) % 4 for d in (1, 2, 3)]
    qs = [(q + d) % 8 for d in (4, 3, 5, 2, 6, 1, 7)]
    core = dev(k=nk)
    dx = [dev(x=v) for v in xs]
    dy = [dev(y=v) for v in ys]
    dz = [dev(z=v) for v in zs]
    dq = [dev(z=v % 4, h=v // 4) for v in qs]
    anti = dev(h=nh)

    sends = []

    def send(src, dst, rsem, target):
        n = len(sends)
        cp = pltpu.make_async_remote_copy(
            src_ref=src, dst_ref=dst, send_sem=ssem.at[n], recv_sem=rsem, device_id=target, device_id_type=MESH
        )
        cp.start()
        sends.append(cp)

    def got(dst, rsem):
        pltpu.make_async_remote_copy(
            src_ref=dst, dst_ref=dst, send_sem=ssem.at[0], recv_sem=rsem, device_id=core, device_id_type=MESH
        ).wait_recv()

    loads = [
        pltpu.make_async_copy(feat, X.at[0, c], lsem.at[0]),
        pltpu.make_async_copy(cot, X.at[1, c], lsem.at[1]),
        pltpu.make_async_copy(vals_hbm.at[pl.ds(0, LIVE)], V.at[pl.ds(0, LIVE)], lsem.at[2]),
        pltpu.make_async_copy(w1_hbm, W1, lsem.at[3]),
        pltpu.make_async_copy(w2_hbm, W2, lsem.at[4]),
    ]
    for cp in loads:
        cp.start()

    barrier = pltpu.get_barrier_semaphore()
    partners = [core] + dx + dy + dq
    for target in partners:
        pl.semaphore_signal(barrier, inc=1, device_id=target, device_id_type=MESH)
    pl.semaphore_wait(barrier, len(partners))

    def slot(h, x, k):
        return h * 8 + x * 2 + k

    def spread(a, s, targets):
        for t in targets:
            send(X.at[a, s], X.at[a, s], rsX.at[a * 16 + s], t)

    def have(a, s):
        got(X.at[a, s], rsX.at[a * 16 + s])

    for a in range(2):
        loads[a].wait()
        spread(a, c, [anti] + dx + [core])

    loads[2].wait()
    V[LIVE] = jnp.zeros((128, 128), BF)
    VT[LIVE] = jnp.zeros((128, 128), BF)

    def flip(s, carry):
        VT[s] = V[s].T
        return carry

    lax.fori_loop(0, LIVE, flip, 0)

    def place(i, carry):
        for j in range(8):
            S[i, :, j * 128 : (j + 1) * 128] = V[table[i * 8 + j]]
            ST[i, :, j * 128 : (j + 1) * 128] = VT[table[j * 8 + i]]
        return carry

    lax.fori_loop(0, 8, place, 0)

    for a in range(2):
        s = slot(nh, x, k)
        have(a, s)
        spread(a, s, dx + [core])

    for a in range(2):
        for hh in (h, nh):
            for v in xs:
                s = slot(hh, v, k)
                have(a, s)
                spread(a, s, [core])
        for hh in (h, nh):
            for v in [x] + xs:
                have(a, slot(hh, v, nk))
        for j in zs + [z]:
            lhs = ST[pl.ds(2 * j, 2)].reshape(256, 1024)
            prod = dot(lhs, X[a].reshape(1024, WIDTH))
            PT[a, j] = prod.astype(BF).reshape(4, ROWS, WIDTH)
            for v, t in zip(ys, dy):
                send(PT.at[a, j, v], RY.at[a, y, j], rsRY.at[a * 16 + y * 4 + j], t)

    def reduce_y(a):
        for j, t in zip(zs + [z], dz + [None]):
            total = PT[a, j, y].astype(F32)
            for v in ys:
                got(RY.at[a, v, j], rsRY.at[a * 16 + v * 4 + j])
                total += RY[a, v, j].astype(F32)
            if t is None:
                KEEP[...] = total
            else:
                Q[a, j] = total.astype(BF)
                send(Q.at[a, j], RZ.at[a, z], rsRZ.at[a * 4 + z], t)

    def reduce_z(a):
        total = KEEP[...]
        for v in zs:
            got(RZ.at[a, v], rsRZ.at[a * 4 + v])
            total += RZ[a, v].astype(F32)
        return total

    reduce_y(0)
    agg = reduce_z(0)
    loads[3].wait()
    loads[4].wait()
    agg_hi = agg.astype(BF)
    agg_lo = (agg - agg_hi.astype(F32)).astype(BF)
    both = dot(jnp.concatenate([agg_hi, agg_lo], axis=0), W1[...])
    v1 = both[:ROWS] + both[ROWS:]
    th = jnp.tanh(GELU_A * (v1 + GELU_B * v1 * v1 * v1))
    act = (0.5 * v1 * (1.0 + th)).astype(BF)
    dact = 0.5 * (1.0 + th) + 0.5 * v1 * (1.0 - th * th) * GELU_A * (1.0 + 3.0 * GELU_B * v1 * v1)
    Y[r] = dot(act, W2[...]).astype(BF)
    for t in dz + dy:
        send(Y.at[r], Y.at[r], rsY.at[r], t)
    ACT[0] = dact
    GB[0, 0] = jnp.where(k == 0, agg_hi, act)
    GB[0, 1] = jnp.where(k == 0, agg_lo, jnp.zeros_like(agg_lo))
    GS[0] = jnp.where(k == 0, act, agg_hi)
    GS[1] = jnp.where(k == 0, jnp.zeros_like(agg_lo), agg_lo)

    reduce_y(1)
    for v in zs:
        s = v * 4 + y
        got(Y.at[s], rsY.at[s])
        for t in dy:
            send(Y.at[s], Y.at[s], rsY.at[s], t)
    bs = reduce_z(1).astype(BF)
    back = lax.dot_general(bs, W2[...], (((1,), (1,)), ((), ())), preferred_element_type=F32)
    bf = (back * ACT[0]).astype(BF)
    GB[0, 2] = jnp.where(k == 0, bf, bs)
    GS[2] = jnp.where(k == 0, bs, bf)
    send(GS, GB.at[1], rsGB.at[0], core)
    got(GB.at[1], rsGB.at[0])

    lhs = jnp.concatenate([GB[0, 0], GB[0, 1], GB[1, 0], GB[1, 1]], axis=0)
    rhs = jnp.concatenate([GB[0, 2], GB[0, 2], GB[1, 2], GB[1, 2]], axis=0)
    terms = lax.dot_general(lhs, rhs, (((0,), (0,)), ((), ())), preferred_element_type=F32)
    TG[...] = terms.reshape(4, 128, WIDTH)
    GT[...] = terms.astype(BF).reshape(4, 128, WIDTH)
    for v, t in zip(xs, dx):
        send(GT.at[v], RGX.at[x], rsRGX.at[x], t)

    for zz in zs + [z]:
        for v in ys:
            s = zz * 4 + v
            got(Y.at[s], rsY.at[s])
    for i in range(4):
        prod = dot(S[pl.ds(2 * i, 2)].reshape(256, 1024), Y[...].reshape(1024, WIDTH))
        PO[pl.ds(4 * i, 4)] = prod.astype(BF).reshape(4, ROWS, WIDTH)
        for g in range(2):
            b = 2 * i + g
            send(PO.at[2 * b + nk], RK.at[b], rsRK.at[b], core)

    for hh in (nh, h):
        for v, t in zip(xs + [x], dx + [None]):
            b = hh * 4 + v
            got(RK.at[b], rsRK.at[b])
            Q2[b] = (PO[2 * b + k].astype(F32) + RK[b].astype(F32)).astype(BF)
            if t is not None:
                send(Q2.at[b], RX.at[x, hh], rsRX.at[x * 2 + hh], t)

    total = TG[x]
    for v in xs:
        got(RGX.at[v], rsRGX.at[v])
        total += RGX[v].astype(F32)
    GY[...] = total.reshape(4, 32, WIDTH)
    for v, t in zip(ys, dy):
        send(GY.at[v], RGY.at[y], rsRGY.at[y], t)

    for hh in (nh, h):
        total = Q2[hh * 4 + x].astype(F32)
        for v in xs:
            got(RX.at[v, hh], rsRX.at[v * 2 + hh])
            total += RX[v, hh].astype(F32)
        if hh is nh:
            Q3[...] = total.astype(BF)
            send(Q3, RH, rsRH.at[0], anti)
        else:
            KEEP[...] = total

    total = GY[y]
    for v in ys:
        got(RGY.at[v], rsRGY.at[v])
        total += RGY[v]
    for i in range(4):
        for j in range(2):
            GZ[2 * i + j] = total[8 * i : 8 * i + 8, 256 * j : 256 * j + 256]
    for v, t in zip(qs, dq):
        send(GZ.at[v], RGZ.at[q], rsRGZ.at[q], t)

    got(RH, rsRH.at[0])
    OUT[...] = (KEEP[...] + RH[...].astype(F32)).astype(BF)
    store_out = pltpu.make_async_copy(OUT, out_hbm, lsem.at[5])
    store_out.start()

    total = GZ[q]
    for v in qs:
        got(RGZ.at[v], rsRGZ.at[v])
        total += RGZ[v]
    FZ[q] = total
    for t in dq:
        send(FZ.at[q], FZ.at[q], rsFZ.at[q], t)
    for v in qs:
        got(FZ.at[v], rsFZ.at[v])
    rows = []
    for i in range(4):
        rows.append(jnp.concatenate([FZ[2 * i], FZ[2 * i + 1]], axis=1))
    FG[k, x, y] = jnp.concatenate(rows, axis=0).astype(BF)
    for t in dy:
        send(FG.at[k, x, y], FG.at[k, x, y], rsFY.at[y], t)
    for v in ys:
        got(FG.at[k, x, v], rsFY.at[v])
    for t in dx + [core]:
        send(FG.at[k, x], FG.at[k, x], rsFX.at[k * 4 + x], t)
    for v in xs:
        got(FG.at[k, v], rsFX.at[k * 4 + v])
        send(FG.at[k, v], FG.at[k, v], rsFX.at[k * 4 + v], core)
    store_own = pltpu.make_async_copy(FG.at[k], grad_hbm.at[k], lsem.at[6])
    store_own.start()
    for v in [x] + xs:
        got(FG.at[nk, v], rsFX.at[nk * 4 + v])
    store_other = pltpu.make_async_copy(FG.at[nk], grad_hbm.at[nk], lsem.at[7])
    store_other.start()
    for cp in sends:
        cp.wait_send()
    store_out.wait()
    store_own.wait()
    store_other.wait()


def local(features, w_first, w_second, block_index, block_count, block_values, cotangent):
    index = block_index[0, 0][:LIVE]
    count = block_count[0, 0]
    ids = jnp.arange(LIVE, dtype=jnp.int32)
    places = jnp.arange(64, dtype=jnp.int32)
    hit = (index[None, :] == places[:, None]) & (ids < count)[None, :]
    table = LIVE + jnp.sum(jnp.where(hit, ids[None, :] - LIVE, 0), axis=1, dtype=jnp.int32)
    anyspace = pl.BlockSpec(memory_space=pl.ANY)
    vm = pltpu.VMEM
    dma = pltpu.SemaphoreType.DMA
    piece = (ROWS, WIDTH)
    out, grads = pl.pallas_call(
        kernel,
        name="gcn",
        out_shape=(
            jax.ShapeDtypeStruct(piece, BF),
            jax.ShapeDtypeStruct((2, 4, 4, 32, WIDTH), BF),
        ),
        in_specs=[pl.BlockSpec(memory_space=pltpu.SMEM)] + [anyspace] * 5,
        out_specs=(anyspace, anyspace),
        scratch_shapes=[
            vm((2, 16) + piece, BF),
            vm((2, 4, 4) + piece, BF),
            vm((2, 4, 4) + piece, BF),
            vm((2, 4) + piece, BF),
            vm((2, 4) + piece, BF),
            vm((16,) + piece, BF),
            vm((16,) + piece, BF),
            vm((8,) + piece, BF),
            vm((8,) + piece, BF),
            vm((4, 2) + piece, BF),
            vm(piece, BF),
            vm(piece, BF),
            vm((8, 128, 1024), BF),
            vm((8, 128, 1024), BF),
            vm((LIVE + 1, 128, 128), BF),
            vm((LIVE + 1, 128, 128), BF),
            vm((WIDTH, WIDTH), BF),
            vm((WIDTH, WIDTH), BF),
            vm((3,) + piece, BF),
            vm((2, 3) + piece, BF),
            vm((4, 128, WIDTH), F32),
            vm((4, 128, WIDTH), BF),
            vm((4, 128, WIDTH), BF),
            vm((4, 32, WIDTH), F32),
            vm((4, 32, WIDTH), F32),
            vm((8, 8, 256), F32),
            vm((8, 8, 256), F32),
            vm((8, 8, 256), F32),
            vm((2, 4, 4, 32, WIDTH), BF),
            vm((1,) + piece, F32),
            vm(piece, BF),
            vm(piece, F32),
            dma((160,)),
            dma((32,)), dma((32,)), dma((8,)), dma((16,)), dma((8,)), dma((8,)), dma((1,)), dma((1,)),
            dma((4,)), dma((4,)), dma((8,)), dma((8,)), dma((4,)), dma((8,)), dma((1,)), dma((8,)),
        ],
        compiler_params=pltpu.CompilerParams(collective_id=0, has_side_effects=True, vmem_limit_bytes=48 << 20),
    )(table, features, cotangent, w_first, w_second, block_values[0, 0])
    grads = grads.reshape(2, WIDTH, WIDTH).astype(F32)
    return out, grads[0], grads[1]


def solution(mesh):
    return jax.shard_map(
        local,
        mesh=mesh,
        in_specs=(
            P(("row", "col"), None),
            P(),
            P(),
            P("row", "col", None),
            P("row", "col"),
            P("row", "col", None, None, None),
            P(("row", "col"), None),
        ),
        out_specs=(P(("row", "col"), None), P(), P()),
        check_vma=False,
    )
```

```python
import jax
import jax.numpy as jnp
from jax import lax
from jax.experimental import pallas as pl
from jax.experimental.pallas import tpu as pltpu
from jax.sharding import PartitionSpec as P

MESH = pl.DeviceIdType.MESH
BF = jnp.bfloat16
F32 = jnp.float32
ROWS = 64
WIDTH = 512
LIVE = 16
GELU_A = 0.7978845608
GELU_B = 0.044715


def dot(a, b):
    return jnp.dot(a, b, preferred_element_type=F32)


NCH = 2
NSEND = 320
CW = 512
HALF = ROWS // 2


def kernel(
    table, feat, cot, w1_hbm, w2_hbm, vals_hbm, out_hbm, grad_hbm,
    X, PT, RA, RB, Q, RZ, KEEP, Y, PO, RK, Q2, OX, Q3, RH, S, ST, V, VT, W1, W2,
    GS, GB, GT, GR, GY, RGY, GZ, RGZ, FZ, FG, ACT, OUT,
    ssem, rsX, rsXH, rsA, rsB, rsRZ, rsY, rsRK, rsOX, rsRH, rsGB, rsGR, rsRGY, rsRGZ,
    rsFZ, rsFY, rsFX, rsFK, lsem,
):
    r = lax.axis_index("row")
    c = lax.axis_index("col")
    z, y = r // 4, r % 4
    h, x, k = c // 8, (c // 2) % 4, c % 2
    q = h * 4 + z
    nh, nk = 1 - h, 1 - k

    def dev(z=z, y=y, h=h, x=x, k=k):
        return (z * 4 + y, h * 8 + x * 2 + k)

    xp, xm, xa = (x + 1) % 4, (x + 3) % 4, (x + 2) % 4
    yp, ym, ya = (y + 1) % 4, (y + 3) % 4, (y + 2) % 4
    zs = [(z + d) % 4 for d in (1, 2, 3)]
    ys = [yp, ym, ya]
    qs = [(q + d) % 8 for d in (4, 3, 5, 2, 6, 1, 7)]
    core = dev(k=nk)
    dxp, dxm = dev(x=xp), dev(x=xm)
    xs = [xp, xm, xa]
    dx = [dxp, dxm, dev(x=xa)]
    dyp, dym = dev(y=yp), dev(y=ym)
    dy = [dyp, dym, dev(y=ya)]
    dz = [dev(z=v) for v in zs]
    dq = [dev(z=v % 4, h=v // 4) for v in qs]
    anti = dev(h=nh)

    sends = []

    def send(src, dst, rsem, target):
        n = len(sends)
        cp = pltpu.make_async_remote_copy(
            src_ref=src, dst_ref=dst, send_sem=ssem.at[n], recv_sem=rsem, device_id=target, device_id_type=MESH
        )
        cp.start()
        sends.append(cp)

    def got(dst, rsem):
        pltpu.make_async_remote_copy(
            src_ref=dst, dst_ref=dst, send_sem=ssem.at[0], recv_sem=rsem, device_id=core, device_id_type=MESH
        ).wait_recv()

    def ring_start(at, p, m, o, up, down, ra, rb, sa, sb, n):
        send(at(o).at[:n], ra.at[0], sa(0), up)
        send(at(o).at[n:], ra.at[1], sa(1), down)
        send(at(p).at[n:], rb.at[0, n:], sb(0), up)
        send(at(m).at[:n], rb.at[1, :n], sb(1), down)

    def ring_relay(at, p, m, up, down, ra, rb, sa, sb, n):
        got(ra.at[0], sa(0))
        at(p)[:n] = (at(p)[:n].astype(F32) + ra[0].astype(F32)).astype(BF)
        send(at(p).at[:n], rb.at[0, :n], sb(2), up)
        got(ra.at[1], sa(1))
        at(m)[n:] = (at(m)[n:].astype(F32) + ra[1].astype(F32)).astype(BF)
        send(at(m).at[n:], rb.at[1, n:], sb(3), down)

    def ring_sum(rb, sb, n):
        got(rb.at[0, n:], sb(0))
        got(rb.at[1, :n], sb(1))
        got(rb.at[0, :n], sb(2))
        got(rb.at[1, n:], sb(3))
        return rb[0].astype(F32) + rb[1].astype(F32)

    loads = []
    for a in range(NCH):
        for i in range(2):
            src = (feat, cot)[a].at[pl.ds(i * HALF, HALF)]
            loads.append(pltpu.make_async_copy(src, X.at[a, c, i], lsem.at[2 * a + i]))
    loads += [
        pltpu.make_async_copy(vals_hbm.at[pl.ds(0, LIVE)], V.at[pl.ds(0, LIVE)], lsem.at[10]),
        pltpu.make_async_copy(w1_hbm, W1, lsem.at[4]),
        pltpu.make_async_copy(w2_hbm, W2, lsem.at[5]),
    ]
    for cp in loads:
        cp.start()

    barrier = pltpu.get_barrier_semaphore()
    partners = [core] + dx + dy + dq
    for target in partners:
        pl.semaphore_signal(barrier, inc=1, device_id=target, device_id_type=MESH)
    pl.semaphore_wait(barrier, len(partners))

    def slot(h, x, k):
        return h * 8 + x * 2 + k

    def spread(a, s, targets, halves=(0, 1)):
        for i in halves if a == 0 else ():
            for t in targets:
                send(X.at[0, s, i], X.at[0, s, i], rsX.at[i * 16 + s], t)
        for t in targets if a == 1 else ():
            send(X.at[1, s], X.at[1, s], rsX.at[32 + s], t)

    def have(a, s, halves=(0, 1)):
        for i in halves if a == 0 else ():
            got(X.at[0, s, i], rsX.at[i * 16 + s])
        if a == 1:
            got(X.at[1, s], rsX.at[32 + s])

    for i in range(2):
        loads[i].wait()
        spread(0, c, [anti], (i,))
    spread(0, c, dx + [core])
    loads[2].wait()
    loads[3].wait()
    spread(1, c, [anti, core])

    loads[4].wait()
    V[LIVE] = jnp.zeros((128, 128), BF)
    VT[LIVE] = jnp.zeros((128, 128), BF)

    def flip(s, carry):
        VT[s] = V[s].T
        return carry

    lax.fori_loop(0, LIVE, flip, 0)

    def place(i, carry):
        for j in range(8):
            S[i, :, j * 128 : (j + 1) * 128] = V[table[i * 8 + j]]
            ST[i, :, j * 128 : (j + 1) * 128] = VT[table[j * 8 + i]]
        return carry

    lax.fori_loop(0, 8, place, 0)

    def across(a, halves=(0, 1)):
        s = slot(nh, x, k)
        for i in halves:
            have(a, s, (i,))
            spread(a, s, (dx if a == 0 else [dxp, dxm]) + [core], (i,))

    def half_sem(hh, i):
        return rsXH.at[hh * 2 + i]

    def near(hh):
        s = slot(hh, xm, k)
        have(1, s)
        send(X.at[1, s, 0], X.at[1, s, 0], half_sem(hh, 0), dxp)
        spread(1, s, [core])
        s = slot(hh, xp, k)
        have(1, s)
        send(X.at[1, s, 1], X.at[1, s, 1], half_sem(hh, 1), dxm)
        spread(1, s, [core])

    def far(hh):
        s = slot(hh, xa, k)
        got(X.at[1, s, 0], half_sem(hh, 0))
        got(X.at[1, s, 1], half_sem(hh, 1))
        spread(1, s, [core])

    def line_in(hh, i):
        for v in xs:
            s = slot(hh, v, k)
            have(0, s, (i,))
            spread(0, s, [core], (i,))

    def y_args(a, j):
        return (
            RA.at[a, j], RB.at[a, j],
            lambda i: rsA.at[a * 8 + j * 2 + i], lambda i: rsB.at[a * 16 + j * 4 + i], HALF,
        )

    order = list(zip(zs + [z], dz + [None]))

    def core_done(a):
        for hh in (h, nh):
            for v in (x, xm, xp, xa):
                have(a, slot(hh, v, nk))

    def start(a, i):
        j = order[i][0]
        lhs = ST[pl.ds(2 * j, 2)].reshape(256, 1024)
        PT[a, j] = dot(lhs, X[a].reshape(1024, CW)).astype(BF).reshape(4, ROWS, CW)
        ring_start(lambda v: PT.at[a, j, v], yp, ym, ya, dyp, dym, *y_args(a, j))

    def relay(a, i):
        j = order[i][0]
        ring_relay(lambda v: PT.at[a, j, v], yp, ym, dyp, dym, *y_args(a, j))

    def reduce_y(a, i):
        j, t = order[i]
        _, rb, _, sb, n = y_args(a, j)
        total = PT[a, j, y].astype(F32) + ring_sum(rb, sb, n)
        if t is None:
            KEEP[a] = total
        else:
            Q[a, j] = total.astype(BF)
            send(Q.at[a, j], RZ.at[a, z], rsRZ.at[a * 4 + z], t)

    def reduce_z(a):
        total = KEEP[a]
        for v in zs:
            got(RZ.at[a, v], rsRZ.at[a * 4 + v])
            total += RZ[a, v].astype(F32)
        return total

    across(0)
    spread(1, c, [dxp, dxm])
    line_in(h, 0)
    line_in(h, 1)
    across(1, (0,))
    line_in(nh, 0)
    line_in(nh, 1)
    core_done(0)
    start(0, 0)
    start(0, 1)
    start(0, 2)
    near(h)
    near(nh)
    relay(0, 0)
    start(0, 3)
    far(h)
    far(nh)
    relay(0, 1)
    core_done(1)
    start(1, 0)
    relay(0, 2)
    reduce_y(0, 0)
    start(1, 1)
    relay(0, 3)
    reduce_y(0, 1)
    start(1, 2)
    relay(1, 0)
    reduce_y(0, 2)
    start(1, 3)
    relay(1, 1)
    reduce_y(0, 3)
    relay(1, 2)
    reduce_y(1, 0)
    relay(1, 3)
    agg = reduce_z(0)
    loads[5].wait()
    loads[6].wait()
    agg_hi = agg.astype(BF)
    agg_lo = (agg - agg_hi.astype(F32)).astype(BF)
    both = dot(jnp.concatenate([agg_hi, agg_lo], axis=0), W1[...])
    v1 = both[:ROWS] + both[ROWS:]
    th = jnp.tanh(GELU_A * (v1 + GELU_B * v1 * v1 * v1))
    act = (0.5 * v1 * (1.0 + th)).astype(BF)
    dact = 0.5 * (1.0 + th) + 0.5 * v1 * (1.0 - th * th) * GELU_A * (1.0 + 3.0 * GELU_B * v1 * v1)
    Y[r] = dot(act, W2[...]).astype(BF)
    ACT[0] = dact
    GB[0, 0] = jnp.where(k == 0, agg_hi, act)
    GB[0, 1] = jnp.where(k == 0, agg_lo, jnp.zeros_like(agg_lo))
    GS[0] = jnp.where(k == 0, act, agg_hi)
    GS[1] = jnp.where(k == 0, jnp.zeros_like(agg_lo), agg_lo)

    reduce_y(1, 1)
    reduce_y(1, 2)
    reduce_y(1, 3)
    for t in dz + dy:
        send(Y.at[r], Y.at[r], rsY.at[r], t)
    bs = reduce_z(1).astype(BF)
    back = lax.dot_general(bs, W2[...], (((1,), (1,)), ((), ())), preferred_element_type=F32)
    bf = (back * ACT[0]).astype(BF)
    GB[0, 2] = jnp.where(k == 0, bf, bs)
    GS[2] = jnp.where(k == 0, bs, bf)
    send(GS, GB.at[1], rsGB.at[0], core)
    def pass_on(i):
        s = zs[i] * 4 + y
        got(Y.at[s], rsY.at[s])
        for t in dy:
            send(Y.at[s], Y.at[s], rsY.at[s], t)

    got(GB.at[1], rsGB.at[0])

    lhs = jnp.concatenate([GB[0, 0], GB[0, 1], GB[1, 0], GB[1, 1]], axis=0)
    rhs = jnp.concatenate([GB[0, 2], GB[0, 2], GB[1, 2], GB[1, 2]], axis=0)
    terms = lax.dot_general(lhs, rhs, (((0,), (0,)), ((), ())), preferred_element_type=F32)
    GT[...] = terms.astype(BF).reshape(4, 128, WIDTH)
    for v, t in zip(xs, dx):
        send(GT.at[v], GR.at[x], rsGR.at[x], t)

    for i in range(3):
        pass_on(i)
    total = GT[x].astype(F32)
    for v in xs:
        got(GR.at[v], rsGR.at[v])
        total += GR[v].astype(F32)
    GY[...] = total.reshape(4, 32, WIDTH)
    for v, t in zip(ys, dy):
        send(GY.at[v], RGY.at[y], rsRGY.at[y], t)
    total = GY[y]
    for v in ys:
        got(RGY.at[v], rsRGY.at[v])
        total += RGY[v]
    for u in range(4):
        for w in range(2):
            GZ[2 * u + w] = total[8 * u : 8 * u + 8, 256 * w : 256 * w + 256]
    for v, t in zip(qs, dq):
        send(GZ.at[v], RGZ.at[q], rsRGZ.at[q], t)

    for zz in zs + [z]:
        for v in ys:
            s = zz * 4 + v
            got(Y.at[s], rsY.at[s])
    def forward(hh):
        for i in range(2):
            prod = dot(S[pl.ds(hh * 4 + 2 * i, 2)].reshape(256, 1024), Y[...].reshape(1024, WIDTH))
            PO[pl.ds(hh * 8 + 4 * i, 4)] = prod.astype(BF).reshape(4, ROWS, WIDTH)
            for g in range(2):
                b = hh * 4 + 2 * i + g
                send(PO.at[2 * b + nk], RK.at[b], rsRK.at[b], core)

    def chip_sum(hh):
        for v, t in zip(xs + [x], dx + [None]):
            b = hh * 4 + v
            got(RK.at[b], rsRK.at[b])
            Q2[b] = (PO[2 * b + k].astype(F32) + RK[b].astype(F32)).astype(BF)
            if t is not None:
                send(Q2.at[b], OX.at[hh, x], rsOX.at[hh * 4 + x], t)

    def x_sum(hh):
        total = Q2[hh * 4 + x].astype(F32)
        for v in xs:
            got(OX.at[hh, v], rsOX.at[hh * 4 + v])
            total += OX[hh, v].astype(F32)
        return total

    forward(nh)
    forward(h)
    chip_sum(nh)
    chip_sum(h)

    total = GZ[q]
    for v in qs:
        got(RGZ.at[v], rsRGZ.at[v])
        total += RGZ[v]
    FZ[q] = total
    for t in dq:
        send(FZ.at[q], FZ.at[q], rsFZ.at[q], t)

    Q3[...] = x_sum(nh).astype(BF)
    send(Q3, RH, rsRH.at[0], anti)
    final = x_sum(h)
    for v in qs:
        got(FZ.at[v], rsFZ.at[v])
    for i in range(2):
        rows = []
        for u in range(2):
            rows.append(jnp.concatenate([FZ[4 * i + 2 * u], FZ[4 * i + 2 * u + 1]], axis=1))
        FG[k, x, y, i] = jnp.concatenate(rows, axis=0).astype(BF)
        for t in (dy, dx)[i]:
            send(FG.at[k, x, y, i], FG.at[k, x, y, i], rsFY.at[i * 4 + (y, x)[i]], t)

    def line(kk, i, v):
        return FG.at[kk, v, :, 0] if i == 0 else FG.at[kk, :, v, 1]

    got(RH, rsRH.at[0])
    OUT[...] = (final + RH[...].astype(F32)).astype(BF)
    store_out = pltpu.make_async_copy(OUT, out_hbm, lsem.at[7])
    store_out.start()
    for i in range(2):
        me = (x, y)[i]
        for v in (ys, xs)[i]:
            got(FG.at[k, x, v, 0] if i == 0 else FG.at[k, v, y, 1], rsFY.at[i * 4 + v])
        for t in (dx, dy)[i]:
            send(line(k, i, me), line(k, i, me), rsFX.at[i * 4 + me], t)
        send(line(k, i, me), line(k, i, me), rsFK.at[i * 4 + me], core)
    for d in range(3):
        for i in range(2):
            v = (xs, ys)[i][d]
            got(line(k, i, v), rsFX.at[i * 4 + v])
            send(line(k, i, v), line(k, i, v), rsFK.at[i * 4 + v], core)
    store_own = pltpu.make_async_copy(FG.at[k], grad_hbm.at[k], lsem.at[8])
    store_own.start()
    for i in range(2):
        for v in range(4):
            got(line(nk, i, v), rsFK.at[i * 4 + v])
    store_other = pltpu.make_async_copy(FG.at[nk], grad_hbm.at[nk], lsem.at[9])
    store_other.start()
    for cp in sends:
        cp.wait_send()
    store_out.wait()
    store_own.wait()
    store_other.wait()


def local(features, w_first, w_second, block_index, block_count, block_values, cotangent):
    index = block_index[0, 0][:LIVE]
    count = block_count[0, 0]
    ids = jnp.arange(LIVE, dtype=jnp.int32)
    places = jnp.arange(64, dtype=jnp.int32)
    hit = (index[None, :] == places[:, None]) & (ids < count)[None, :]
    table = LIVE + jnp.sum(jnp.where(hit, ids[None, :] - LIVE, 0), axis=1, dtype=jnp.int32)
    anyspace = pl.BlockSpec(memory_space=pl.ANY)
    vm = pltpu.VMEM
    dma = pltpu.SemaphoreType.DMA
    piece = (ROWS, WIDTH)
    chunk = (ROWS, CW)
    out, grads = pl.pallas_call(
        kernel,
        name="gcn",
        out_shape=(
            jax.ShapeDtypeStruct(piece, BF),
            jax.ShapeDtypeStruct((2, 4, 4, 2, 16, WIDTH), BF),
        ),
        in_specs=[pl.BlockSpec(memory_space=pltpu.SMEM)] + [anyspace] * 5,
        out_specs=(anyspace, anyspace),
        scratch_shapes=[
            vm((2, 16, 2, HALF, WIDTH), BF),
            vm((NCH, 4, 4) + chunk, BF),
            vm((NCH, 4, 2, HALF, CW), BF),
            vm((NCH, 4, 2) + chunk, BF),
            vm((NCH, 4) + chunk, BF),
            vm((NCH, 4) + chunk, BF),
            vm((NCH,) + chunk, F32),
            vm((16,) + piece, BF),
            vm((16,) + piece, BF),
            vm((8,) + piece, BF),
            vm((8,) + piece, BF),
            vm((2, 4) + piece, BF),
            vm(piece, BF),
            vm(piece, BF),
            vm((8, 128, 1024), BF),
            vm((8, 128, 1024), BF),
            vm((LIVE + 1, 128, 128), BF),
            vm((LIVE + 1, 128, 128), BF),
            vm((WIDTH, WIDTH), BF),
            vm((WIDTH, WIDTH), BF),
            vm((3,) + piece, BF),
            vm((2, 3) + piece, BF),
            vm((4, 128, WIDTH), BF),
            vm((4, 128, WIDTH), BF),
            vm((4, 32, WIDTH), F32),
            vm((4, 32, WIDTH), F32),
            vm((8, 8, 256), F32),
            vm((8, 8, 256), F32),
            vm((8, 8, 256), F32),
            vm((2, 4, 4, 2, 16, WIDTH), BF),
            vm((1,) + piece, F32),
            vm(piece, BF),
            dma((NSEND,)),
            dma((48,)),
            dma((4,)),
            dma((8 * NCH,)),
            dma((16 * NCH,)),
            dma((4 * NCH,)),
            dma((16,)),
            dma((8,)),
            dma((8,)),
            dma((1,)),
            dma((1,)),
            dma((4,)),
            dma((4,)),
            dma((8,)),
            dma((8,)),
            dma((8,)),
            dma((8,)),
            dma((8,)),
            dma((11,)),
        ],
        compiler_params=pltpu.CompilerParams(collective_id=0, has_side_effects=True),
    )(table, features, cotangent, w_first, w_second, block_values[0, 0])
    grads = grads.reshape(2, WIDTH, WIDTH).astype(F32)
    return out, grads[0], grads[1]


def solution(mesh):
    return jax.shard_map(
        local,
        mesh=mesh,
        in_specs=(
            P(("row", "col"), None),
            P(),
            P(),
            P("row", "col", None),
            P("row", "col"),
            P("row", "col", None, None, None),
            P(("row", "col"), None),
        ),
        out_specs=(P(("row", "col"), None), P(), P()),
        check_vma=False,
    )
```

```python
import jax
import jax.numpy as jnp
from jax import lax
from jax.experimental import pallas as pl
from jax.experimental.pallas import tpu as pltpu
from jax.sharding import PartitionSpec as P

MESH = pl.DeviceIdType.MESH
BF = jnp.bfloat16
F32 = jnp.float32
ROWS = 64
WIDTH = 512
LIVE = 16
GELU_A = 0.7978845608
GELU_B = 0.044715


def dot(a, b):
    return jnp.dot(a, b, preferred_element_type=F32)


NCH = 2
NSEND = 360
CW = 512
HALF = ROWS // 2
PART = WIDTH // 2


def kernel(
    index_hbm, count_hbm, feat, cot, w1_hbm, w2_hbm, vals_hbm, out_hbm, grad_hbm,
    X, PT, RA, RB, RD, Q, RZ, KEEP, Y, PO, RK, Q2, OX, Q3, RH, S, ST, V, VT, W1, W2,
    index, count, table, GS, GB, GT, GR, GF, GY, RGY, GZ, RGZ, FZ, FG, ACT, OUT,
    ssem, rsX, rsXH, rsA, rsB, rsD, rsRZ, rsY, rsRK, rsOX, rsRH, rsGB, rsGR, rsRGY, rsRGZ,
    rsFZ, rsFY, rsFX, rsFK, lsem,
):
    r = lax.axis_index("row")
    c = lax.axis_index("col")
    z, y = r // 4, r % 4
    h, x, k = c // 8, (c // 2) % 4, c % 2
    q = h * 4 + z
    nh, nk = 1 - h, 1 - k

    def dev(z=z, y=y, h=h, x=x, k=k):
        return (z * 4 + y, h * 8 + x * 2 + k)

    xp, xm, xa = (x + 1) % 4, (x + 3) % 4, (x + 2) % 4
    yp, ym, ya = (y + 1) % 4, (y + 3) % 4, (y + 2) % 4
    zfar, znear = 3 * (1 - z // 2), 1 + z % 2
    zs = [zfar, 6 - z - zfar - znear, znear]
    ys = [yp, ym, ya]
    qs = [(q + d) % 8 for d in (4, 3, 5, 2, 6, 1, 7)]
    core = dev(k=nk)
    dxp, dxm = dev(x=xp), dev(x=xm)
    xs = [xp, xm, xa]
    dx = [dxp, dxm, dev(x=xa)]
    dyp, dym = dev(y=yp), dev(y=ym)
    dy = [dyp, dym, dev(y=ya)]
    dz = [dev(z=v) for v in zs]
    dq = [dev(z=v % 4, h=v // 4) for v in qs]
    anti = dev(h=nh)

    sends = []

    def send(src, dst, rsem, target):
        n = len(sends)
        cp = pltpu.make_async_remote_copy(
            src_ref=src, dst_ref=dst, send_sem=ssem.at[n], recv_sem=rsem, device_id=target, device_id_type=MESH
        )
        cp.start()
        sends.append(cp)

    def got(dst, rsem):
        pltpu.make_async_remote_copy(
            src_ref=dst, dst_ref=dst, send_sem=ssem.at[0], recv_sem=rsem, device_id=core, device_id_type=MESH
        ).wait_recv()

    def ring_start(at, p, m, o, up, down, ra, rb, sa, sb, n):
        send(at(o).at[:n], ra.at[0], sa(0), up)
        send(at(o).at[n:], ra.at[1], sa(1), down)
        send(at(p).at[n:], rb.at[0, n:], sb(0), up)
        send(at(m).at[:n], rb.at[1, :n], sb(1), down)

    def ring_relay(at, p, m, up, down, ra, rb, sa, sb, n):
        got(ra.at[0], sa(0))
        at(p)[:n] = (at(p)[:n].astype(F32) + ra[0].astype(F32)).astype(BF)
        send(at(p).at[:n], rb.at[0, :n], sb(2), up)
        got(ra.at[1], sa(1))
        at(m)[n:] = (at(m)[n:].astype(F32) + ra[1].astype(F32)).astype(BF)
        send(at(m).at[n:], rb.at[1, n:], sb(3), down)

    def ring_sum(rb, sb, n):
        got(rb.at[0, n:], sb(0))
        got(rb.at[1, :n], sb(1))
        got(rb.at[0, :n], sb(2))
        got(rb.at[1, n:], sb(3))
        return rb[0].astype(F32) + rb[1].astype(F32)

    loads = []
    for a in range(NCH):
        for i in range(2):
            src = (feat, cot)[a].at[pl.ds(i * HALF, HALF)]
            loads.append(pltpu.make_async_copy(src, X.at[a, c, i], lsem.at[2 * a + i]))
    loads += [
        pltpu.make_async_copy(vals_hbm.at[pl.ds(0, LIVE)], V.at[pl.ds(0, LIVE)], lsem.at[10]),
        pltpu.make_async_copy(index_hbm, index, lsem.at[6]),
        pltpu.make_async_copy(count_hbm, count, lsem.at[7]),
        pltpu.make_async_copy(w1_hbm, W1, lsem.at[4]),
        pltpu.make_async_copy(w2_hbm, W2, lsem.at[5]),
    ]
    for cp in loads:
        cp.start()

    barrier = pltpu.get_barrier_semaphore()
    partners = [core] + dx + dy + dq
    for target in partners:
        pl.semaphore_signal(barrier, inc=1, device_id=target, device_id_type=MESH)
    pl.semaphore_wait(barrier, len(partners))

    def slot(h, x, k):
        return h * 8 + x * 2 + k

    def spread(a, s, targets, halves=(0, 1)):
        for i in halves if a == 0 else ():
            for t in targets:
                send(X.at[0, s, i], X.at[0, s, i], rsX.at[i * 16 + s], t)
        for t in targets if a == 1 else ():
            send(X.at[1, s], X.at[1, s], rsX.at[32 + s], t)

    def have(a, s, halves=(0, 1)):
        for i in halves if a == 0 else ():
            got(X.at[0, s, i], rsX.at[i * 16 + s])
        if a == 1:
            got(X.at[1, s], rsX.at[32 + s])

    for i in range(2):
        loads[i].wait()
        spread(0, c, [anti], (i,))
    spread(0, c, dx + [core])
    loads[2].wait()
    loads[3].wait()
    spread(1, c, [anti, core])

    loads[5].wait()
    loads[6].wait()
    ids = [index[s] for s in range(LIVE)]
    live = [s < count[0, 0] for s in range(LIVE)]

    def find(p, carry):
        at = jnp.int32(LIVE)
        for s in range(LIVE):
            at = jnp.where((ids[s] == p) & live[s], jnp.int32(s), at)
        table[p] = at
        return carry

    lax.fori_loop(0, 64, find, 0)
    loads[4].wait()
    V[LIVE] = jnp.zeros((128, 128), BF)
    VT[LIVE] = jnp.zeros((128, 128), BF)

    def flip(s, carry):
        VT[s] = V[s].T
        return carry

    lax.fori_loop(0, LIVE, flip, 0)

    def place(i, carry):
        for j in range(8):
            S[i, :, j * 128 : (j + 1) * 128] = V[table[i * 8 + j]]
            ST[i, :, j * 128 : (j + 1) * 128] = VT[table[j * 8 + i]]
        return carry

    lax.fori_loop(0, 8, place, 0)

    def across(a, halves=(0, 1)):
        s = slot(nh, x, k)
        for i in halves:
            have(a, s, (i,))
            spread(a, s, (dx if a == 0 else [dxp, dxm]) + [core], (i,))

    def half_sem(hh, i):
        return rsXH.at[hh * 2 + i]

    def near(hh):
        s = slot(hh, xm, k)
        have(1, s)
        send(X.at[1, s, 0], X.at[1, s, 0], half_sem(hh, 0), dxp)
        spread(1, s, [core])
        s = slot(hh, xp, k)
        have(1, s)
        send(X.at[1, s, 1], X.at[1, s, 1], half_sem(hh, 1), dxm)
        spread(1, s, [core])

    def far(hh):
        s = slot(hh, xa, k)
        got(X.at[1, s, 0], half_sem(hh, 0))
        got(X.at[1, s, 1], half_sem(hh, 1))
        spread(1, s, [core])

    def line_in(hh, i):
        for v in xs:
            s = slot(hh, v, k)
            have(0, s, (i,))
            spread(0, s, [core], (i,))

    def y_args(a, j):
        return (
            RA.at[a, j], RB.at[a, j],
            lambda i: rsA.at[a * 8 + j * 2 + i], lambda i: rsB.at[a * 16 + j * 4 + i], HALF,
        )

    order = list(zip(zs + [z], dz + [None]))

    def core_done(a):
        for hh in (h, nh):
            for v in (x, xm, xp, xa):
                have(a, slot(hh, v, nk))

    def straight(a, i):
        return a == 1 and i == 3

    def start(a, i):
        j = order[i][0]
        lhs = ST[pl.ds(2 * j, 2)].reshape(256, 1024)
        PT[a, j] = dot(lhs, X[a].reshape(1024, CW)).astype(BF).reshape(4, ROWS, CW)
        if not straight(a, i):
            ring_start(lambda v: PT.at[a, j, v], yp, ym, ya, dyp, dym, *y_args(a, j))

    def relay(a, i):
        j = order[i][0]
        ring_relay(lambda v: PT.at[a, j, v], yp, ym, dyp, dym, *y_args(a, j))

    def reduce_y(a, i):
        j, t = order[i]
        _, rb, _, sb, n = y_args(a, j)
        total = PT[a, j, y].astype(F32)
        if straight(a, i):
            for v in ys:
                got(RD.at[v], rsD.at[v])
                total += RD[v].astype(F32)
        else:
            total += ring_sum(rb, sb, n)
        if t is None:
            KEEP[a] = total
        else:
            Q[a, j] = total.astype(BF)
            send(Q.at[a, j], RZ.at[a, z], rsRZ.at[a * 4 + z], t)

    def reduce_z(a):
        total = KEEP[a]
        for v in zs:
            got(RZ.at[a, v], rsRZ.at[a * 4 + v])
            total += RZ[a, v].astype(F32)
        return total

    across(0)
    spread(1, c, [dxp, dxm])
    line_in(h, 0)
    line_in(h, 1)
    across(1, (0,))
    line_in(nh, 0)
    line_in(nh, 1)
    core_done(0)
    start(0, 0)
    start(0, 1)
    start(0, 2)
    near(h)
    near(nh)
    relay(0, 0)
    start(0, 3)
    far(h)
    far(nh)
    relay(0, 1)
    core_done(1)
    start(1, 0)
    relay(0, 2)
    reduce_y(0, 0)
    start(1, 1)
    relay(0, 3)
    reduce_y(0, 1)
    start(1, 2)
    relay(1, 0)
    reduce_y(0, 2)
    start(1, 3)
    relay(1, 1)
    reduce_y(0, 3)
    relay(1, 2)
    for v, t in zip(ys, dy):
        send(PT.at[1, z, v], RD.at[y], rsD.at[y], t)
    reduce_y(1, 0)
    agg = reduce_z(0)
    loads[7].wait()
    loads[8].wait()
    agg_hi = agg.astype(BF)
    agg_lo = (agg - agg_hi.astype(F32)).astype(BF)
    both = dot(jnp.concatenate([agg_hi, agg_lo], axis=0), W1[...])
    v1 = both[:ROWS] + both[ROWS:]
    th = jnp.tanh(GELU_A * (v1 + GELU_B * v1 * v1 * v1))
    act = (0.5 * v1 * (1.0 + th)).astype(BF)
    dact = 0.5 * (1.0 + th) + 0.5 * v1 * (1.0 - th * th) * GELU_A * (1.0 + 3.0 * GELU_B * v1 * v1)
    linear = dot(act, W2[...]).astype(BF)
    for e in range(2):
        Y[e, r] = linear[:, e * PART : (e + 1) * PART]
    ACT[0] = dact
    GB[0, 0] = jnp.where(k == 0, agg_hi, act)
    GB[0, 1] = jnp.where(k == 0, agg_lo, jnp.zeros_like(agg_lo))
    GS[0] = jnp.where(k == 0, act, agg_hi)
    GS[1] = jnp.where(k == 0, jnp.zeros_like(agg_lo), agg_lo)

    reduce_y(1, 1)
    reduce_y(1, 2)
    reduce_y(1, 3)
    bs = reduce_z(1).astype(BF)
    back = lax.dot_general(bs, W2[...], (((1,), (1,)), ((), ())), preferred_element_type=F32)
    bf = (back * ACT[0]).astype(BF)
    GB[0, 2] = jnp.where(k == 0, bf, bs)
    GS[2] = jnp.where(k == 0, bs, bf)
    send(GS, GB.at[1], rsGB.at[0], core)
    for e in range(2):
        for t in dz:
            send(Y.at[e, r], Y.at[e, r], rsY.at[e * 16 + r], t)

    def pass_on(e):
        for v in zs:
            s = v * 4 + y
            got(Y.at[e, s], rsY.at[e * 16 + s])
            for t in dy:
                send(Y.at[e, s], Y.at[e, s], rsY.at[e * 16 + s], t)

    got(GB.at[1], rsGB.at[0])

    lhs = jnp.concatenate([GB[0, 0], GB[0, 1], GB[1, 0], GB[1, 1]], axis=0)
    rhs = jnp.concatenate([GB[0, 2], GB[0, 2], GB[1, 2], GB[1, 2]], axis=0)
    terms = lax.dot_general(lhs, rhs, (((0,), (0,)), ((), ())), preferred_element_type=F32)
    GT[...] = terms.astype(BF).reshape(2, 4, ROWS, WIDTH)
    sides = ((x, xs, dx), (y, ys, dy))
    for i in range(2):
        me, others, devs = sides[i]
        for v, t in zip(others, devs):
            send(GT.at[i, v], GR.at[i, me], rsGR.at[i * 4 + me], t)

    for e in range(2):
        for t in dy:
            send(Y.at[e, r], Y.at[e, r], rsY.at[e * 16 + r], t)
    for i in range(2):
        me, others, _ = sides[i]
        total = GT[i, me].astype(F32)
        for v in others:
            got(GR.at[i, v], rsGR.at[i * 4 + v])
            total += GR[i, v].astype(F32)
        GF[i] = total.reshape(4, 16, WIDTH)
        GY[i] = total.astype(BF).reshape(4, 16, WIDTH)
        me, others, devs = sides[1 - i]
        for v, t in zip(others, devs):
            send(GY.at[i, v], RGY.at[i, me], rsRGY.at[i * 4 + me], t)
    pass_on(0)
    pass_on(1)
    for i in range(2):
        me, others, _ = sides[1 - i]
        total = GF[i, me]
        for v in others:
            got(RGY.at[i, v], rsRGY.at[i * 4 + v])
            total += RGY[i, v].astype(F32)
        for w in range(4):
            GZ[4 * i + w] = total[:, 128 * w : 128 * w + 128]
    for v, t in zip(qs, dq):
        send(GZ.at[v], RGZ.at[q], rsRGZ.at[q], t)

    def forward(e):
        for zz in zs + [z]:
            for v in ys:
                s = zz * 4 + v
                got(Y.at[e, s], rsY.at[e * 16 + s])
        for i in range(2):
            prod = dot(S[pl.ds(4 * i, 4)].reshape(512, 1024), Y[e].reshape(1024, PART))
            PO[e, pl.ds(8 * i, 8)] = prod.astype(BF).reshape(8, ROWS, PART)
            for g in range(4):
                b = 4 * i + g
                send(PO.at[e, 2 * b + nk], RK.at[e, b], rsRK.at[e * 8 + b], core)

    def chip_sum(e):
        for hh in (nh, h):
            for v, t in zip(xs + [x], dx + [None]):
                b = hh * 4 + v
                got(RK.at[e, b], rsRK.at[e * 8 + b])
                Q2[e, b] = (PO[e, 2 * b + k].astype(F32) + RK[e, b].astype(F32)).astype(BF)
                if t is not None:
                    send(Q2.at[e, b], OX.at[e, hh, x], rsOX.at[e * 8 + hh * 4 + x], t)

    def x_sum(e):
        sums = []
        for hh in (nh, h):
            total = Q2[e, hh * 4 + x].astype(F32)
            for v in xs:
                got(OX.at[e, hh, v], rsOX.at[e * 8 + hh * 4 + v])
                total += OX[e, hh, v].astype(F32)
            if hh is nh:
                Q3[e] = total.astype(BF)
                send(Q3.at[e], RH.at[e], rsRH.at[e], anti)
        return total

    def finish(e, total):
        got(RH.at[e], rsRH.at[e])
        OUT[:, e * PART : (e + 1) * PART] = (total + RH[e].astype(F32)).astype(BF)

    forward(0)
    total = GZ[q]
    for v in qs:
        got(RGZ.at[v], rsRGZ.at[v])
        total += RGZ[v]
    FZ[q] = total.astype(BF)
    for t in dq:
        send(FZ.at[q], FZ.at[q], rsFZ.at[q], t)
    chip_sum(0)
    forward(1)

    for v in qs:
        got(FZ.at[v], rsFZ.at[v])
    for i in range(2):
        outer, inner = (x, y) if i == 0 else (y, x)
        FG[k, i, outer, inner] = jnp.concatenate([FZ[4 * i + w] for w in range(4)], axis=1)
        for t in sides[1 - i][2]:
            send(FG.at[k, i, outer, inner], FG.at[k, i, outer, inner], rsFY.at[i * 4 + inner], t)

    chip_sum(1)
    first_half = x_sum(0)
    for i in range(2):
        me, _, devs = sides[i]
        for v in sides[1 - i][1]:
            got(FG.at[k, i, me, v], rsFY.at[i * 4 + v])
        for t in devs:
            send(FG.at[k, i, me], FG.at[k, i, me], rsFX.at[i * 4 + me], t)
        send(FG.at[k, i, me], FG.at[k, i, me], rsFK.at[i * 4 + me], core)

    stores = []

    def store(kk, i, v):
        cp = pltpu.make_async_copy(FG.at[kk, i, v], grad_hbm.at[kk, i, v], lsem.at[len(stores)])
        cp.start()
        stores.append(cp)

    second_half = x_sum(1)
    finish(0, first_half)
    for d in range(3):
        for i in range(2):
            v = sides[i][1][d]
            got(FG.at[k, i, v], rsFX.at[i * 4 + v])
            send(FG.at[k, i, v], FG.at[k, i, v], rsFK.at[i * 4 + v], core)
    for i in range(2):
        for v in range(4):
            store(k, i, v)
    for i in range(2):
        for v in (sides[i][0], *sides[i][1]):
            got(FG.at[nk, i, v], rsFK.at[i * 4 + v])
            store(nk, i, v)
    finish(1, second_half)
    store_out = pltpu.make_async_copy(OUT, out_hbm, lsem.at[16])
    store_out.start()
    for cp in sends:
        cp.wait_send()
    store_out.wait()
    for cp in stores:
        cp.wait()


def local(features, w_first, w_second, block_index, block_count, block_values, cotangent):
    anyspace = pl.BlockSpec(memory_space=pl.ANY)
    vm = pltpu.VMEM
    dma = pltpu.SemaphoreType.DMA
    piece = (ROWS, WIDTH)
    chunk = (ROWS, CW)
    part = (ROWS, PART)
    out, grads = pl.pallas_call(
        kernel,
        name="gcn",
        out_shape=(
            jax.ShapeDtypeStruct(piece, BF),
            jax.ShapeDtypeStruct((2, 2, 4, 4, 16, WIDTH), BF),
        ),
        in_specs=[anyspace] * 7,
        out_specs=(anyspace, anyspace),
        scratch_shapes=[
            vm((2, 16, 2, HALF, WIDTH), BF),
            vm((NCH, 4, 4) + chunk, BF),
            vm((NCH, 4, 2, HALF, CW), BF),
            vm((NCH, 4, 2) + chunk, BF),
            vm((4,) + piece, BF),
            vm((NCH, 4) + chunk, BF),
            vm((NCH, 4) + chunk, BF),
            vm((NCH,) + chunk, F32),
            vm((2, 16) + part, BF),
            vm((2, 16) + part, BF),
            vm((2, 8) + part, BF),
            vm((2, 8) + part, BF),
            vm((2, 2, 4) + part, BF),
            vm((2,) + part, BF),
            vm((2,) + part, BF),
            vm((8, 128, 1024), BF),
            vm((8, 128, 1024), BF),
            vm((LIVE + 1, 128, 128), BF),
            vm((LIVE + 1, 128, 128), BF),
            vm((WIDTH, WIDTH), BF),
            vm((WIDTH, WIDTH), BF),
            pltpu.SMEM((64,), jnp.int32),
            pltpu.SMEM((1, 1), jnp.int32),
            pltpu.SMEM((64,), jnp.int32),
            vm((3,) + piece, BF),
            vm((2, 3) + piece, BF),
            vm((2, 4) + piece, BF),
            vm((2, 4) + piece, BF),
            vm((2, 4, 16, WIDTH), F32),
            vm((2, 4, 16, WIDTH), BF),
            vm((2, 4, 16, WIDTH), BF),
            vm((8, 16, 128), F32),
            vm((8, 16, 128), F32),
            vm((8, 16, 128), BF),
            vm((2, 2, 4, 4, 16, WIDTH), BF),
            vm((1,) + piece, F32),
            vm(piece, BF),
            dma((NSEND,)),
            dma((48,)),
            dma((4,)),
            dma((8 * NCH,)),
            dma((16 * NCH,)),
            dma((4,)),
            dma((4 * NCH,)),
            dma((32,)),
            dma((16,)),
            dma((16,)),
            dma((2,)),
            dma((1,)),
            dma((8,)),
            dma((8,)),
            dma((8,)),
            dma((8,)),
            dma((8,)),
            dma((8,)),
            dma((8,)),
            dma((17,)),
        ],
        compiler_params=pltpu.CompilerParams(collective_id=0, has_side_effects=True),
    )(block_index[0, 0], block_count, features, cotangent, w_first, w_second, block_values[0, 0])
    grads = grads.reshape(2, WIDTH, WIDTH).astype(F32)
    return out, grads[0], grads[1]


def solution(mesh):
    return jax.shard_map(
        local,
        mesh=mesh,
        in_specs=(
            P(("row", "col"), None),
            P(),
            P(),
            P("row", "col", None),
            P("row", "col"),
            P("row", "col", None, None, None),
            P(("row", "col"), None),
        ),
        out_specs=(P(("row", "col"), None), P(), P()),
        check_vma=False,
    )
```

```python
import jax
import jax.numpy as jnp
from jax import lax
from jax.experimental import pallas as pl
from jax.experimental.pallas import tpu as pltpu
from jax.sharding import PartitionSpec as P

MESH = pl.DeviceIdType.MESH
BF = jnp.bfloat16
F32 = jnp.float32
ROWS = 64
WIDTH = 512
LIVE = 16
GELU_A = 0.7978845608
GELU_B = 0.044715


def dot(a, b):
    return jnp.dot(a, b, preferred_element_type=F32)


NCH = 2
NSEND = 360
CW = 512
HALF = ROWS // 2
PART = WIDTH // 2


def kernel(
    index_hbm, count_hbm, feat, cot, w1_hbm, w2_hbm, vals_hbm, out_hbm, grad_hbm,
    X, PT, RA, RB, RD, Q, RZ, KEEP, Y, PO, RK, Q2, OX, Q3, RH, S, ST, V, VT, W1, W2,
    index, count, table, GS, GB, GT, GR, GF, GY, RGY, GZ, RGZ, FZ, FG, ACT, OUT,
    ssem, rsX, rsXH, rsA, rsB, rsD, rsRZ, rsY, rsRK, rsOX, rsRH, rsGB, rsGR, rsRGY, rsRGZ,
    rsFZ, rsFY, rsFX, rsFK, lsem,
):
    r = lax.axis_index("row")
    c = lax.axis_index("col")
    z, y = r // 4, r % 4
    h, x, k = c // 8, (c // 2) % 4, c % 2
    q = h * 4 + z
    nh, nk = 1 - h, 1 - k

    def dev(z=z, y=y, h=h, x=x, k=k):
        return (z * 4 + y, h * 8 + x * 2 + k)

    xp, xm, xa = (x + 1) % 4, (x + 3) % 4, (x + 2) % 4
    yp, ym, ya = (y + 1) % 4, (y + 3) % 4, (y + 2) % 4
    zfar, znear = 3 * (1 - z // 2), 1 + z % 2
    zs = [zfar, 6 - z - zfar - znear, znear]
    ys = [yp, ym, ya]
    qs = [(q + d) % 8 for d in (4, 3, 5, 2, 6, 1, 7)]
    core = dev(k=nk)
    dxp, dxm = dev(x=xp), dev(x=xm)
    xs = [xp, xm, xa]
    dx = [dxp, dxm, dev(x=xa)]
    dyp, dym = dev(y=yp), dev(y=ym)
    dy = [dyp, dym, dev(y=ya)]
    dz = [dev(z=v) for v in zs]
    dq = [dev(z=v % 4, h=v // 4) for v in qs]
    anti = dev(h=nh)

    sends = []

    def send(src, dst, rsem, target):
        n = len(sends)
        cp = pltpu.make_async_remote_copy(
            src_ref=src, dst_ref=dst, send_sem=ssem.at[n], recv_sem=rsem, device_id=target, device_id_type=MESH
        )
        cp.start()
        sends.append(cp)

    def got(dst, rsem):
        pltpu.make_async_remote_copy(
            src_ref=dst, dst_ref=dst, send_sem=ssem.at[0], recv_sem=rsem, device_id=core, device_id_type=MESH
        ).wait_recv()

    def ring_start(at, p, m, o, up, down, ra, rb, sa, sb, n):
        send(at(o).at[:n], ra.at[0], sa(0), up)
        send(at(o).at[n:], ra.at[1], sa(1), down)
        send(at(p).at[n:], rb.at[0, n:], sb(0), up)
        send(at(m).at[:n], rb.at[1, :n], sb(1), down)

    def ring_relay(at, p, m, up, down, ra, rb, sa, sb, n):
        got(ra.at[0], sa(0))
        at(p)[:n] = (at(p)[:n].astype(F32) + ra[0].astype(F32)).astype(BF)
        send(at(p).at[:n], rb.at[0, :n], sb(2), up)
        got(ra.at[1], sa(1))
        at(m)[n:] = (at(m)[n:].astype(F32) + ra[1].astype(F32)).astype(BF)
        send(at(m).at[n:], rb.at[1, n:], sb(3), down)

    def ring_sum(rb, sb, n):
        got(rb.at[0, n:], sb(0))
        got(rb.at[1, :n], sb(1))
        got(rb.at[0, :n], sb(2))
        got(rb.at[1, n:], sb(3))
        return rb[0].astype(F32) + rb[1].astype(F32)

    loads = []
    for a in range(NCH):
        for i in range(2):
            src = (feat, cot)[a].at[pl.ds(i * HALF, HALF)]
            loads.append(pltpu.make_async_copy(src, X.at[a, c, i], lsem.at[2 * a + i]))
    loads += [
        pltpu.make_async_copy(vals_hbm.at[pl.ds(0, LIVE)], V.at[pl.ds(0, LIVE)], lsem.at[10]),
        pltpu.make_async_copy(index_hbm, index, lsem.at[6]),
        pltpu.make_async_copy(count_hbm, count, lsem.at[7]),
        pltpu.make_async_copy(w1_hbm, W1, lsem.at[4]),
        pltpu.make_async_copy(w2_hbm, W2, lsem.at[5]),
    ]
    for cp in loads:
        cp.start()

    barrier = pltpu.get_barrier_semaphore()
    partners = [core] + dx + dy + dq
    for target in partners:
        pl.semaphore_signal(barrier, inc=1, device_id=target, device_id_type=MESH)
    pl.semaphore_wait(barrier, len(partners))

    def slot(h, x, k):
        return h * 8 + x * 2 + k

    def spread(a, s, targets, halves=(0, 1)):
        for i in halves if a == 0 else ():
            for t in targets:
                send(X.at[0, s, i], X.at[0, s, i], rsX.at[i * 16 + s], t)
        for t in targets if a == 1 else ():
            send(X.at[1, s], X.at[1, s], rsX.at[32 + s], t)

    def have(a, s, halves=(0, 1)):
        for i in halves if a == 0 else ():
            got(X.at[0, s, i], rsX.at[i * 16 + s])
        if a == 1:
            got(X.at[1, s], rsX.at[32 + s])

    for i in range(2):
        loads[i].wait()
        spread(0, c, [anti], (i,))
    spread(0, c, dx + [core])
    loads[2].wait()
    loads[3].wait()
    spread(1, c, [anti, core])

    loads[5].wait()
    loads[6].wait()
    ids = [index[s] for s in range(LIVE)]
    live = [s < count[0, 0] for s in range(LIVE)]

    def find(p, carry):
        at = jnp.int32(LIVE)
        for s in range(LIVE):
            at = jnp.where((ids[s] == p) & live[s], jnp.int32(s), at)
        table[p] = at
        return carry

    lax.fori_loop(0, 64, find, 0)
    loads[4].wait()
    V[LIVE] = jnp.zeros((128, 128), BF)
    VT[LIVE] = jnp.zeros((128, 128), BF)

    def flip(s, carry):
        VT[s] = V[s].T
        return carry

    lax.fori_loop(0, LIVE, flip, 0)

    def place(i, carry):
        for j in range(8):
            S[i, :, j * 128 : (j + 1) * 128] = V[table[i * 8 + j]]
            ST[i, :, j * 128 : (j + 1) * 128] = VT[table[j * 8 + i]]
        return carry

    lax.fori_loop(0, 8, place, 0)

    def across(a, halves=(0, 1)):
        s = slot(nh, x, k)
        for i in halves:
            have(a, s, (i,))
            spread(a, s, (dx if a == 0 else [dxp, dxm]) + [core], (i,))

    def half_sem(hh, i):
        return rsXH.at[hh * 2 + i]

    def near(hh):
        s = slot(hh, xm, k)
        have(1, s)
        send(X.at[1, s, 0], X.at[1, s, 0], half_sem(hh, 0), dxp)
        spread(1, s, [core])
        s = slot(hh, xp, k)
        have(1, s)
        send(X.at[1, s, 1], X.at[1, s, 1], half_sem(hh, 1), dxm)
        spread(1, s, [core])

    def far(hh):
        s = slot(hh, xa, k)
        got(X.at[1, s, 0], half_sem(hh, 0))
        got(X.at[1, s, 1], half_sem(hh, 1))
        spread(1, s, [core])

    def line_in(hh, i):
        for v in xs:
            s = slot(hh, v, k)
            have(0, s, (i,))
            spread(0, s, [core], (i,))

    def y_args(a, j):
        return (
            RA.at[a, j], RB.at[a, j],
            lambda i: rsA.at[a * 8 + j * 2 + i], lambda i: rsB.at[a * 16 + j * 4 + i], HALF,
        )

    order = list(zip(zs + [z], dz + [None]))

    def core_done(a):
        for hh in (h, nh):
            for v in (x, xm, xp, xa):
                have(a, slot(hh, v, nk))

    def straight(a, i):
        return a == 1 and i == 3

    def start(a, i):
        j = order[i][0]
        lhs = ST[pl.ds(2 * j, 2)].reshape(256, 1024)
        PT[a, j] = dot(lhs, X[a].reshape(1024, CW)).astype(BF).reshape(4, ROWS, CW)
        if not straight(a, i):
            ring_start(lambda v: PT.at[a, j, v], yp, ym, ya, dyp, dym, *y_args(a, j))

    def relay(a, i):
        j = order[i][0]
        ring_relay(lambda v: PT.at[a, j, v], yp, ym, dyp, dym, *y_args(a, j))

    def reduce_y(a, i):
        j, t = order[i]
        _, rb, _, sb, n = y_args(a, j)
        total = PT[a, j, y].astype(F32)
        if straight(a, i):
            for v in ys:
                got(RD.at[v], rsD.at[v])
                total += RD[v].astype(F32)
        else:
            total += ring_sum(rb, sb, n)
        if t is None:
            KEEP[a] = total
        else:
            Q[a, j] = total.astype(BF)
            send(Q.at[a, j], RZ.at[a, z], rsRZ.at[a * 4 + z], t)

    def reduce_z(a):
        total = KEEP[a]
        for v in zs:
            got(RZ.at[a, v], rsRZ.at[a * 4 + v])
            total += RZ[a, v].astype(F32)
        return total

    across(0)
    spread(1, c, [dxp, dxm])
    line_in(h, 0)
    line_in(h, 1)
    across(1, (0,))
    line_in(nh, 0)
    line_in(nh, 1)
    core_done(0)
    start(0, 0)
    start(0, 1)
    start(0, 2)
    near(h)
    near(nh)
    relay(0, 0)
    start(0, 3)
    far(h)
    far(nh)
    relay(0, 1)
    core_done(1)
    start(1, 0)
    relay(0, 2)
    reduce_y(0, 0)
    start(1, 1)
    relay(0, 3)
    reduce_y(0, 1)
    relay(1, 0)
    start(1, 2)
    reduce_y(0, 2)
    start(1, 3)
    relay(1, 1)
    relay(1, 2)
    for v, t in zip(ys, dy):
        send(PT.at[1, z, v], RD.at[y], rsD.at[y], t)
    reduce_y(1, 0)
    reduce_y(1, 1)
    reduce_y(1, 2)
    reduce_y(0, 3)
    agg = reduce_z(0)
    loads[7].wait()
    loads[8].wait()
    agg_hi = agg.astype(BF)
    agg_lo = (agg - agg_hi.astype(F32)).astype(BF)
    both = dot(jnp.concatenate([agg_hi, agg_lo], axis=0), W1[...])
    v1 = both[:ROWS] + both[ROWS:]
    th = jnp.tanh(GELU_A * (v1 + GELU_B * v1 * v1 * v1))
    act = (0.5 * v1 * (1.0 + th)).astype(BF)
    dact = 0.5 * (1.0 + th) + 0.5 * v1 * (1.0 - th * th) * GELU_A * (1.0 + 3.0 * GELU_B * v1 * v1)
    linear = dot(act, W2[...]).astype(BF)
    for e in range(2):
        Y[e, r] = linear[:, e * PART : (e + 1) * PART]
    ACT[0] = dact
    GB[0, 0] = jnp.where(k == 0, agg_hi, act)
    GB[0, 1] = jnp.where(k == 0, agg_lo, jnp.zeros_like(agg_lo))
    GS[0] = jnp.where(k == 0, act, agg_hi)
    GS[1] = jnp.where(k == 0, jnp.zeros_like(agg_lo), agg_lo)
    send(GS.at[:2], GB.at[1, :2], rsGB.at[1], core)

    reduce_y(1, 3)
    bs = reduce_z(1).astype(BF)
    back = lax.dot_general(bs, W2[...], (((1,), (1,)), ((), ())), preferred_element_type=F32)
    bf = (back * ACT[0]).astype(BF)
    GB[0, 2] = jnp.where(k == 0, bf, bs)
    GS[2] = jnp.where(k == 0, bs, bf)
    send(GS.at[2], GB.at[1, 2], rsGB.at[0], core)
    for e in range(2):
        for t in dz:
            send(Y.at[e, r], Y.at[e, r], rsY.at[e * 16 + r], t)

    def pass_on(e):
        for v in zs:
            s = v * 4 + y
            got(Y.at[e, s], rsY.at[e * 16 + s])
            for t in dy:
                send(Y.at[e, s], Y.at[e, s], rsY.at[e * 16 + s], t)

    got(GB.at[1, :2], rsGB.at[1])
    got(GB.at[1, 2], rsGB.at[0])

    lhs = jnp.concatenate([GB[0, 0], GB[0, 1], GB[1, 0], GB[1, 1]], axis=0)
    rhs = jnp.concatenate([GB[0, 2], GB[0, 2], GB[1, 2], GB[1, 2]], axis=0)
    terms = lax.dot_general(lhs, rhs, (((0,), (0,)), ((), ())), preferred_element_type=F32)
    GT[...] = terms.astype(BF).reshape(2, 4, ROWS, WIDTH)
    sides = ((x, xs, dx), (y, ys, dy))
    for i in range(2):
        me, others, devs = sides[i]
        for v, t in zip(others, devs):
            send(GT.at[i, v], GR.at[i, me], rsGR.at[i * 4 + me], t)

    for e in range(2):
        for t in dy:
            send(Y.at[e, r], Y.at[e, r], rsY.at[e * 16 + r], t)
    for i in range(2):
        me, others, _ = sides[i]
        total = GT[i, me].astype(F32)
        for v in others:
            got(GR.at[i, v], rsGR.at[i * 4 + v])
            total += GR[i, v].astype(F32)
        GF[i] = total.reshape(4, 16, WIDTH)
        GY[i] = total.astype(BF).reshape(4, 16, WIDTH)
        me, others, devs = sides[1 - i]
        for v, t in zip(others, devs):
            send(GY.at[i, v], RGY.at[i, me], rsRGY.at[i * 4 + me], t)
    pass_on(0)
    pass_on(1)
    for i in range(2):
        me, others, _ = sides[1 - i]
        total = GF[i, me]
        for v in others:
            got(RGY.at[i, v], rsRGY.at[i * 4 + v])
            total += RGY[i, v].astype(F32)
        for w in range(4):
            GZ[4 * i + w] = total[:, 128 * w : 128 * w + 128]
    for v, t in zip(qs, dq):
        send(GZ.at[v], RGZ.at[q], rsRGZ.at[q], t)

    def forward(e):
        for zz in zs + [z]:
            for v in ys:
                s = zz * 4 + v
                got(Y.at[e, s], rsY.at[e * 16 + s])
        for i in range(2):
            prod = dot(S[pl.ds(4 * i, 4)].reshape(512, 1024), Y[e].reshape(1024, PART))
            PO[e, pl.ds(8 * i, 8)] = prod.astype(BF).reshape(8, ROWS, PART)
            for g in range(4):
                b = 4 * i + g
                send(PO.at[e, 2 * b + nk], RK.at[e, b], rsRK.at[e * 8 + b], core)

    def chip_sum(e):
        for hh in (nh, h):
            for v, t in zip(xs + [x], dx + [None]):
                b = hh * 4 + v
                got(RK.at[e, b], rsRK.at[e * 8 + b])
                Q2[e, b] = (PO[e, 2 * b + k].astype(F32) + RK[e, b].astype(F32)).astype(BF)
                if t is not None:
                    send(Q2.at[e, b], OX.at[e, hh, x], rsOX.at[e * 8 + hh * 4 + x], t)

    def x_sum(e):
        sums = []
        for hh in (nh, h):
            total = Q2[e, hh * 4 + x].astype(F32)
            for v in xs:
                got(OX.at[e, hh, v], rsOX.at[e * 8 + hh * 4 + v])
                total += OX[e, hh, v].astype(F32)
            if hh is nh:
                Q3[e] = total.astype(BF)
                send(Q3.at[e], RH.at[e], rsRH.at[e], anti)
        return total

    def finish(e, total):
        got(RH.at[e], rsRH.at[e])
        OUT[:, e * PART : (e + 1) * PART] = (total + RH[e].astype(F32)).astype(BF)

    total = GZ[q]
    for v in qs:
        got(RGZ.at[v], rsRGZ.at[v])
        total += RGZ[v]
    FZ[q] = total.astype(BF)
    for t in dq:
        send(FZ.at[q], FZ.at[q], rsFZ.at[q], t)
    forward(0)
    chip_sum(0)

    for v in qs:
        got(FZ.at[v], rsFZ.at[v])
    for i in range(2):
        outer, inner = (x, y) if i == 0 else (y, x)
        FG[k, i, outer, inner] = jnp.concatenate([FZ[4 * i + w] for w in range(4)], axis=1)
        for t in sides[1 - i][2]:
            send(FG.at[k, i, outer, inner], FG.at[k, i, outer, inner], rsFY.at[i * 4 + inner], t)

    forward(1)
    chip_sum(1)
    for i in range(2):
        me, _, devs = sides[i]
        for v in sides[1 - i][1]:
            got(FG.at[k, i, me, v], rsFY.at[i * 4 + v])
        for t in devs:
            send(FG.at[k, i, me], FG.at[k, i, me], rsFX.at[i * 4 + me], t)
        send(FG.at[k, i, me], FG.at[k, i, me], rsFK.at[i * 4 + me], core)

    stores = []

    def store(kk, i, v):
        cp = pltpu.make_async_copy(FG.at[kk, i, v], grad_hbm.at[kk, i, v], lsem.at[len(stores)])
        cp.start()
        stores.append(cp)

    first_half = x_sum(0)
    second_half = x_sum(1)
    finish(0, first_half)
    for d in range(3):
        for i in range(2):
            v = sides[i][1][d]
            got(FG.at[k, i, v], rsFX.at[i * 4 + v])
            send(FG.at[k, i, v], FG.at[k, i, v], rsFK.at[i * 4 + v], core)
    for i in range(2):
        for v in range(4):
            store(k, i, v)
    for i in range(2):
        for v in (sides[i][0], *sides[i][1]):
            got(FG.at[nk, i, v], rsFK.at[i * 4 + v])
            store(nk, i, v)
    finish(1, second_half)
    store_out = pltpu.make_async_copy(OUT, out_hbm, lsem.at[16])
    store_out.start()
    for cp in sends:
        cp.wait_send()
    store_out.wait()
    for cp in stores:
        cp.wait()


def local(features, w_first, w_second, block_index, block_count, block_values, cotangent):
    anyspace = pl.BlockSpec(memory_space=pl.ANY)
    vm = pltpu.VMEM
    dma = pltpu.SemaphoreType.DMA
    piece = (ROWS, WIDTH)
    chunk = (ROWS, CW)
    part = (ROWS, PART)
    out, grads = pl.pallas_call(
        kernel,
        name="gcn",
        out_shape=(
            jax.ShapeDtypeStruct(piece, BF),
            jax.ShapeDtypeStruct((2, 2, 4, 4, 16, WIDTH), BF),
        ),
        in_specs=[anyspace] * 7,
        out_specs=(anyspace, anyspace),
        scratch_shapes=[
            vm((2, 16, 2, HALF, WIDTH), BF),
            vm((NCH, 4, 4) + chunk, BF),
            vm((NCH, 4, 2, HALF, CW), BF),
            vm((NCH, 4, 2) + chunk, BF),
            vm((4,) + piece, BF),
            vm((NCH, 4) + chunk, BF),
            vm((NCH, 4) + chunk, BF),
            vm((NCH,) + chunk, F32),
            vm((2, 16) + part, BF),
            vm((2, 16) + part, BF),
            vm((2, 8) + part, BF),
            vm((2, 8) + part, BF),
            vm((2, 2, 4) + part, BF),
            vm((2,) + part, BF),
            vm((2,) + part, BF),
            vm((8, 128, 1024), BF),
            vm((8, 128, 1024), BF),
            vm((LIVE + 1, 128, 128), BF),
            vm((LIVE + 1, 128, 128), BF),
            vm((WIDTH, WIDTH), BF),
            vm((WIDTH, WIDTH), BF),
            pltpu.SMEM((64,), jnp.int32),
            pltpu.SMEM((1, 1), jnp.int32),
            pltpu.SMEM((64,), jnp.int32),
            vm((3,) + piece, BF),
            vm((2, 3) + piece, BF),
            vm((2, 4) + piece, BF),
            vm((2, 4) + piece, BF),
            vm((2, 4, 16, WIDTH), F32),
            vm((2, 4, 16, WIDTH), BF),
            vm((2, 4, 16, WIDTH), BF),
            vm((8, 16, 128), F32),
            vm((8, 16, 128), F32),
            vm((8, 16, 128), BF),
            vm((2, 2, 4, 4, 16, WIDTH), BF),
            vm((1,) + piece, F32),
            vm(piece, BF),
            dma((NSEND,)),
            dma((48,)),
            dma((4,)),
            dma((8 * NCH,)),
            dma((16 * NCH,)),
            dma((4,)),
            dma((4 * NCH,)),
            dma((32,)),
            dma((16,)),
            dma((16,)),
            dma((2,)),
            dma((2,)),
            dma((8,)),
            dma((8,)),
            dma((8,)),
            dma((8,)),
            dma((8,)),
            dma((8,)),
            dma((8,)),
            dma((17,)),
        ],
        compiler_params=pltpu.CompilerParams(collective_id=0, has_side_effects=True),
    )(block_index[0, 0], block_count, features, cotangent, w_first, w_second, block_values[0, 0])
    grads = grads.reshape(2, WIDTH, WIDTH).astype(F32)
    return out, grads[0], grads[1]


def solution(mesh):
    return jax.shard_map(
        local,
        mesh=mesh,
        in_specs=(
            P(("row", "col"), None),
            P(),
            P(),
            P("row", "col", None),
            P("row", "col"),
            P("row", "col", None, None, None),
            P(("row", "col"), None),
        ),
        out_specs=(P(("row", "col"), None), P(), P()),
        check_vma=False,
    )
```

```python
import jax
import jax.numpy as jnp
from jax import lax
from jax.experimental import pallas as pl
from jax.experimental.pallas import tpu as pltpu
from jax.sharding import PartitionSpec as P

MESH = pl.DeviceIdType.MESH
BF = jnp.bfloat16
F32 = jnp.float32
ROWS = 64
WIDTH = 512
LIVE = 16
GELU_A = 0.7978845608
GELU_B = 0.044715


def dot(a, b):
    return jnp.dot(a, b, preferred_element_type=F32)


NCH = 2
NSEND = 360
CW = 512
HALF = ROWS // 2
PART = WIDTH // 2


def kernel(
    index_hbm, count_hbm, feat, cot, w1_hbm, w2_hbm, vals_hbm, out_hbm, grad_hbm,
    X, PT, RA, RB, RD, Q, RZ, KEEP, Y, PO, RK, Q2, OX, Q3, RH, S, ST, V, VT, W1, W2,
    index, count, table, GS, GB, GT, GR, GF, GY, RGY, GZ, RGZ, FZ, FG, ACT, OUT,
    ssem, rsX, rsXH, rsA, rsB, rsD, rsRZ, rsY, rsRK, rsOX, rsRH, rsGB, rsGR, rsRGY, rsRGZ,
    rsFZ, rsFY, rsFX, rsFK, lsem,
):
    r = lax.axis_index("row")
    c = lax.axis_index("col")
    z, y = r // 4, r % 4
    h, x, k = c // 8, (c // 2) % 4, c % 2
    q = h * 4 + z
    nh, nk = 1 - h, 1 - k

    def dev(z=z, y=y, h=h, x=x, k=k):
        return (z * 4 + y, h * 8 + x * 2 + k)

    xp, xm, xa = (x + 1) % 4, (x + 3) % 4, (x + 2) % 4
    yp, ym, ya = (y + 1) % 4, (y + 3) % 4, (y + 2) % 4
    zfar, znear = 3 * (1 - z // 2), 1 + z % 2
    zs = [zfar, 6 - z - zfar - znear, znear]
    ys = [yp, ym, ya]
    qs = [(q + d) % 8 for d in (4, 3, 5, 2, 6, 1, 7)]
    core = dev(k=nk)
    dxp, dxm = dev(x=xp), dev(x=xm)
    xs = [xp, xm, xa]
    dx = [dxp, dxm, dev(x=xa)]
    dyp, dym = dev(y=yp), dev(y=ym)
    dy = [dyp, dym, dev(y=ya)]
    dz = [dev(z=v) for v in zs]
    dq = [dev(z=v % 4, h=v // 4) for v in qs]
    anti = dev(h=nh)

    sends = []

    def send(src, dst, rsem, target):
        n = len(sends)
        cp = pltpu.make_async_remote_copy(
            src_ref=src, dst_ref=dst, send_sem=ssem.at[n], recv_sem=rsem, device_id=target, device_id_type=MESH
        )
        cp.start()
        sends.append(cp)

    def got(dst, rsem):
        pltpu.make_async_remote_copy(
            src_ref=dst, dst_ref=dst, send_sem=ssem.at[0], recv_sem=rsem, device_id=core, device_id_type=MESH
        ).wait_recv()

    def ring_start(at, p, m, o, up, down, ra, rb, sa, sb, n):
        send(at(o).at[:n], ra.at[0], sa(0), up)
        send(at(o).at[n:], ra.at[1], sa(1), down)
        send(at(p).at[n:], rb.at[0, n:], sb(0), up)
        send(at(m).at[:n], rb.at[1, :n], sb(1), down)

    def ring_relay(at, p, m, up, down, ra, rb, sa, sb, n):
        got(ra.at[0], sa(0))
        at(p)[:n] = (at(p)[:n].astype(F32) + ra[0].astype(F32)).astype(BF)
        send(at(p).at[:n], rb.at[0, :n], sb(2), up)
        got(ra.at[1], sa(1))
        at(m)[n:] = (at(m)[n:].astype(F32) + ra[1].astype(F32)).astype(BF)
        send(at(m).at[n:], rb.at[1, n:], sb(3), down)

    def ring_sum(rb, sb, n):
        got(rb.at[0, n:], sb(0))
        got(rb.at[1, :n], sb(1))
        got(rb.at[0, :n], sb(2))
        got(rb.at[1, n:], sb(3))
        return rb[0].astype(F32) + rb[1].astype(F32)

    loads = []
    for a in range(NCH):
        for i in range(2):
            src = (feat, cot)[a].at[pl.ds(i * HALF, HALF)]
            loads.append(pltpu.make_async_copy(src, X.at[a, c, i], lsem.at[2 * a + i]))
    loads += [
        pltpu.make_async_copy(vals_hbm.at[pl.ds(0, LIVE)], V.at[pl.ds(0, LIVE)], lsem.at[10]),
        pltpu.make_async_copy(index_hbm, index, lsem.at[6]),
        pltpu.make_async_copy(count_hbm, count, lsem.at[7]),
        pltpu.make_async_copy(w1_hbm, W1, lsem.at[4]),
        pltpu.make_async_copy(w2_hbm, W2, lsem.at[5]),
    ]
    for cp in loads:
        cp.start()

    barrier = pltpu.get_barrier_semaphore()
    partners = [core] + dx + dy + dq
    for target in partners:
        pl.semaphore_signal(barrier, inc=1, device_id=target, device_id_type=MESH)
    pl.semaphore_wait(barrier, len(partners))

    def slot(h, x, k):
        return h * 8 + x * 2 + k

    def spread(a, s, targets, halves=(0, 1)):
        for i in halves if a == 0 else ():
            for t in targets:
                send(X.at[0, s, i], X.at[0, s, i], rsX.at[i * 16 + s], t)
        for t in targets if a == 1 else ():
            send(X.at[1, s], X.at[1, s], rsX.at[32 + s], t)

    def have(a, s, halves=(0, 1)):
        for i in halves if a == 0 else ():
            got(X.at[0, s, i], rsX.at[i * 16 + s])
        if a == 1:
            got(X.at[1, s], rsX.at[32 + s])

    for i in range(2):
        loads[i].wait()
        spread(0, c, [anti], (i,))
    spread(0, c, dx + [core])
    loads[2].wait()
    loads[3].wait()
    spread(1, c, [anti, core])

    loads[5].wait()
    loads[6].wait()
    ids = [index[s] for s in range(LIVE)]
    live = [s < count[0, 0] for s in range(LIVE)]

    def find(p, carry):
        at = jnp.int32(LIVE)
        for s in range(LIVE):
            at = jnp.where((ids[s] == p) & live[s], jnp.int32(s), at)
        table[p] = at
        return carry

    lax.fori_loop(0, 64, find, 0)
    loads[4].wait()
    V[LIVE] = jnp.zeros((128, 128), BF)
    VT[LIVE] = jnp.zeros((128, 128), BF)

    def flip(s, carry):
        VT[s] = V[s].T
        return carry

    lax.fori_loop(0, LIVE, flip, 0)

    def place(i, carry):
        for j in range(8):
            S[i, :, j * 128 : (j + 1) * 128] = V[table[i * 8 + j]]
            ST[i, :, j * 128 : (j + 1) * 128] = VT[table[j * 8 + i]]
        return carry

    lax.fori_loop(0, 8, place, 0)

    def across(a, halves=(0, 1)):
        s = slot(nh, x, k)
        for i in halves:
            have(a, s, (i,))
            spread(a, s, (dx if a == 0 else [dxp, dxm]) + [core], (i,))

    def half_sem(hh, i):
        return rsXH.at[hh * 2 + i]

    def near(hh):
        s = slot(hh, xm, k)
        have(1, s)
        send(X.at[1, s, 0], X.at[1, s, 0], half_sem(hh, 0), dxp)
        spread(1, s, [core])
        s = slot(hh, xp, k)
        have(1, s)
        send(X.at[1, s, 1], X.at[1, s, 1], half_sem(hh, 1), dxm)
        spread(1, s, [core])

    def far(hh):
        s = slot(hh, xa, k)
        got(X.at[1, s, 0], half_sem(hh, 0))
        got(X.at[1, s, 1], half_sem(hh, 1))
        spread(1, s, [core])

    def line_in(hh, i):
        for v in xs:
            s = slot(hh, v, k)
            have(0, s, (i,))
            spread(0, s, [core], (i,))

    def y_args(a, j):
        return (
            RA.at[a, j], RB.at[a, j],
            lambda i: rsA.at[a * 8 + j * 2 + i], lambda i: rsB.at[a * 16 + j * 4 + i], HALF,
        )

    order = list(zip(zs + [z], dz + [None]))

    def core_done(a):
        for hh in (h, nh):
            for v in (x, xm, xp, xa):
                have(a, slot(hh, v, nk))

    def straight(a, i):
        return a == 1 and i == 3

    def start(a, i):
        j = order[i][0]
        lhs = ST[pl.ds(2 * j, 2)].reshape(256, 1024)
        PT[a, j] = dot(lhs, X[a].reshape(1024, CW)).astype(BF).reshape(4, ROWS, CW)
        if not straight(a, i):
            ring_start(lambda v: PT.at[a, j, v], yp, ym, ya, dyp, dym, *y_args(a, j))

    def relay(a, i):
        j = order[i][0]
        ring_relay(lambda v: PT.at[a, j, v], yp, ym, dyp, dym, *y_args(a, j))

    def reduce_y(a, i):
        j, t = order[i]
        _, rb, _, sb, n = y_args(a, j)
        total = PT[a, j, y].astype(F32)
        if straight(a, i):
            for v in ys:
                got(RD.at[v], rsD.at[v])
                total += RD[v].astype(F32)
        else:
            total += ring_sum(rb, sb, n)
        if t is None:
            KEEP[a] = total
        else:
            Q[a, j] = total.astype(BF)
            send(Q.at[a, j], RZ.at[a, z], rsRZ.at[a * 4 + z], t)

    def reduce_z(a):
        total = KEEP[a]
        for v in zs:
            got(RZ.at[a, v], rsRZ.at[a * 4 + v])
            total += RZ[a, v].astype(F32)
        return total

    across(0)
    spread(1, c, [dxp, dxm])
    line_in(h, 0)
    line_in(h, 1)
    across(1, (0,))
    line_in(nh, 0)
    line_in(nh, 1)
    core_done(0)
    start(0, 0)
    start(0, 1)
    start(0, 2)
    near(h)
    near(nh)
    relay(0, 0)
    start(0, 3)
    far(h)
    far(nh)
    relay(0, 1)
    core_done(1)
    start(1, 0)
    relay(0, 2)
    reduce_y(0, 0)
    start(1, 1)
    relay(0, 3)
    reduce_y(0, 1)
    relay(1, 0)
    start(1, 2)
    reduce_y(0, 2)
    start(1, 3)
    relay(1, 1)
    relay(1, 2)
    for v, t in zip(ys, dy):
        send(PT.at[1, z, v], RD.at[y], rsD.at[y], t)
    reduce_y(1, 0)
    reduce_y(1, 1)
    reduce_y(1, 2)
    reduce_y(0, 3)
    agg = reduce_z(0)
    loads[7].wait()
    loads[8].wait()
    agg_hi = agg.astype(BF)
    agg_lo = (agg - agg_hi.astype(F32)).astype(BF)
    both = dot(jnp.concatenate([agg_hi, agg_lo], axis=0), W1[...])
    v1 = both[:ROWS] + both[ROWS:]
    th = jnp.tanh(GELU_A * (v1 + GELU_B * v1 * v1 * v1))
    act = (0.5 * v1 * (1.0 + th)).astype(BF)
    dact = 0.5 * (1.0 + th) + 0.5 * v1 * (1.0 - th * th) * GELU_A * (1.0 + 3.0 * GELU_B * v1 * v1)
    linear = dot(act, W2[...]).astype(BF)
    for e in range(2):
        Y[e, r] = linear[:, e * PART : (e + 1) * PART]
    ACT[0] = dact
    GB[0, 0] = jnp.where(k == 0, agg_hi, act)
    GB[0, 1] = jnp.where(k == 0, agg_lo, jnp.zeros_like(agg_lo))
    GS[0] = jnp.where(k == 0, act, agg_hi)
    GS[1] = jnp.where(k == 0, jnp.zeros_like(agg_lo), agg_lo)
    send(GS.at[:2], GB.at[1, :2], rsGB.at[1], core)

    reduce_y(1, 3)
    bs = reduce_z(1).astype(BF)
    back = lax.dot_general(bs, W2[...], (((1,), (1,)), ((), ())), preferred_element_type=F32)
    bf = (back * ACT[0]).astype(BF)
    GB[0, 2] = jnp.where(k == 0, bf, bs)
    GS[2] = jnp.where(k == 0, bs, bf)
    send(GS.at[2], GB.at[1, 2], rsGB.at[0], core)
    for e in range(2):
        for t in dz:
            send(Y.at[e, r], Y.at[e, r], rsY.at[e * 16 + r], t)

    def pass_on(e):
        for v in zs:
            s = v * 4 + y
            got(Y.at[e, s], rsY.at[e * 16 + s])
            for t in dy:
                send(Y.at[e, s], Y.at[e, s], rsY.at[e * 16 + s], t)

    got(GB.at[1, :2], rsGB.at[1])
    got(GB.at[1, 2], rsGB.at[0])

    lhs = jnp.concatenate([GB[0, 0], GB[0, 1], GB[1, 0], GB[1, 1]], axis=0)
    rhs = jnp.concatenate([GB[0, 2], GB[0, 2], GB[1, 2], GB[1, 2]], axis=0)
    sides = ((x, xs, dx), (y, ys, dy))
    for i in range(2):
        terms = lax.dot_general(
            lhs[:, 256 * i : 256 * i + 256], rhs, (((0,), (0,)), ((), ())), preferred_element_type=F32
        )
        GT[i] = terms.astype(BF).reshape(4, ROWS, WIDTH)
        me, others, devs = sides[i]
        for v, t in zip(others, devs):
            send(GT.at[i, v], GR.at[i, me], rsGR.at[i * 4 + me], t)

    for e in range(2):
        for t in dy:
            send(Y.at[e, r], Y.at[e, r], rsY.at[e * 16 + r], t)
    for i in range(2):
        me, others, _ = sides[i]
        total = GT[i, me].astype(F32)
        for v in others:
            got(GR.at[i, v], rsGR.at[i * 4 + v])
            total += GR[i, v].astype(F32)
        GF[i] = total.reshape(4, 16, WIDTH)
        GY[i] = total.astype(BF).reshape(4, 16, WIDTH)
        me, others, devs = sides[1 - i]
        for v, t in zip(others, devs):
            send(GY.at[i, v], RGY.at[i, me], rsRGY.at[i * 4 + me], t)
    pass_on(0)
    pass_on(1)
    for i in range(2):
        me, others, _ = sides[1 - i]
        total = GF[i, me]
        for v in others:
            got(RGY.at[i, v], rsRGY.at[i * 4 + v])
            total += RGY[i, v].astype(F32)
        for w in range(4):
            GZ[4 * i + w] = total[:, 128 * w : 128 * w + 128].astype(BF)
    for v, t in zip(qs, dq):
        send(GZ.at[v], RGZ.at[q], rsRGZ.at[q], t)

    def forward(e):
        for zz in zs + [z]:
            for v in ys:
                s = zz * 4 + v
                got(Y.at[e, s], rsY.at[e * 16 + s])
        for i in range(2):
            prod = dot(S[pl.ds(4 * i, 4)].reshape(512, 1024), Y[e].reshape(1024, PART))
            PO[e, pl.ds(8 * i, 8)] = prod.astype(BF).reshape(8, ROWS, PART)
            for g in range(4):
                b = 4 * i + g
                send(PO.at[e, 2 * b + nk], RK.at[e, b], rsRK.at[e * 8 + b], core)

    def chip_sum(e):
        for hh in (nh, h):
            for v, t in zip(xs + [x], dx + [None]):
                b = hh * 4 + v
                got(RK.at[e, b], rsRK.at[e * 8 + b])
                Q2[e, b] = (PO[e, 2 * b + k].astype(F32) + RK[e, b].astype(F32)).astype(BF)
                if t is not None:
                    send(Q2.at[e, b], OX.at[e, hh, x], rsOX.at[e * 8 + hh * 4 + x], t)

    def x_sum(e):
        sums = []
        for hh in (nh, h):
            total = Q2[e, hh * 4 + x].astype(F32)
            for v in xs:
                got(OX.at[e, hh, v], rsOX.at[e * 8 + hh * 4 + v])
                total += OX[e, hh, v].astype(F32)
            if hh is nh:
                Q3[e] = total.astype(BF)
                send(Q3.at[e], RH.at[e], rsRH.at[e], anti)
        return total

    def finish(e, total):
        got(RH.at[e], rsRH.at[e])
        OUT[:, e * PART : (e + 1) * PART] = (total + RH[e].astype(F32)).astype(BF)

    total = GZ[q].astype(F32)
    for v in qs:
        got(RGZ.at[v], rsRGZ.at[v])
        total += RGZ[v].astype(F32)
    FZ[q] = total.astype(BF)
    for t in dq:
        send(FZ.at[q], FZ.at[q], rsFZ.at[q], t)
    forward(0)
    chip_sum(0)

    for v in qs:
        got(FZ.at[v], rsFZ.at[v])
    for i in range(2):
        outer, inner = (x, y) if i == 0 else (y, x)
        FG[k, i, outer, inner] = jnp.concatenate([FZ[4 * i + w] for w in range(4)], axis=1)
        for t in sides[1 - i][2]:
            send(FG.at[k, i, outer, inner], FG.at[k, i, outer, inner], rsFY.at[i * 4 + inner], t)

    forward(1)
    chip_sum(1)
    for i in range(2):
        me, _, devs = sides[i]
        for v in sides[1 - i][1]:
            got(FG.at[k, i, me, v], rsFY.at[i * 4 + v])
        for t in devs:
            send(FG.at[k, i, me], FG.at[k, i, me], rsFX.at[i * 4 + me], t)
        send(FG.at[k, i, me], FG.at[k, i, me], rsFK.at[i * 4 + me], core)

    stores = []

    def store(kk, i, v):
        cp = pltpu.make_async_copy(FG.at[kk, i, v], grad_hbm.at[kk, i, v], lsem.at[len(stores)])
        cp.start()
        stores.append(cp)

    first_half = x_sum(0)
    second_half = x_sum(1)
    finish(0, first_half)
    for d in range(3):
        for i in range(2):
            v = sides[i][1][d]
            got(FG.at[k, i, v], rsFX.at[i * 4 + v])
            send(FG.at[k, i, v], FG.at[k, i, v], rsFK.at[i * 4 + v], core)
    for i in range(2):
        for v in range(4):
            store(k, i, v)
    for i in range(2):
        for v in (sides[i][0], *sides[i][1]):
            got(FG.at[nk, i, v], rsFK.at[i * 4 + v])
            store(nk, i, v)
    finish(1, second_half)
    store_out = pltpu.make_async_copy(OUT, out_hbm, lsem.at[16])
    store_out.start()
    for cp in sends:
        cp.wait_send()
    store_out.wait()
    for cp in stores:
        cp.wait()


def local(features, w_first, w_second, block_index, block_count, block_values, cotangent):
    anyspace = pl.BlockSpec(memory_space=pl.ANY)
    vm = pltpu.VMEM
    dma = pltpu.SemaphoreType.DMA
    piece = (ROWS, WIDTH)
    chunk = (ROWS, CW)
    part = (ROWS, PART)
    out, grads = pl.pallas_call(
        kernel,
        name="gcn",
        out_shape=(
            jax.ShapeDtypeStruct(piece, BF),
            jax.ShapeDtypeStruct((2, 2, 4, 4, 16, WIDTH), BF),
        ),
        in_specs=[anyspace] * 7,
        out_specs=(anyspace, anyspace),
        scratch_shapes=[
            vm((2, 16, 2, HALF, WIDTH), BF),
            vm((NCH, 4, 4) + chunk, BF),
            vm((NCH, 4, 2, HALF, CW), BF),
            vm((NCH, 4, 2) + chunk, BF),
            vm((4,) + piece, BF),
            vm((NCH, 4) + chunk, BF),
            vm((NCH, 4) + chunk, BF),
            vm((NCH,) + chunk, F32),
            vm((2, 16) + part, BF),
            vm((2, 16) + part, BF),
            vm((2, 8) + part, BF),
            vm((2, 8) + part, BF),
            vm((2, 2, 4) + part, BF),
            vm((2,) + part, BF),
            vm((2,) + part, BF),
            vm((8, 128, 1024), BF),
            vm((8, 128, 1024), BF),
            vm((LIVE + 1, 128, 128), BF),
            vm((LIVE + 1, 128, 128), BF),
            vm((WIDTH, WIDTH), BF),
            vm((WIDTH, WIDTH), BF),
            pltpu.SMEM((64,), jnp.int32),
            pltpu.SMEM((1, 1), jnp.int32),
            pltpu.SMEM((64,), jnp.int32),
            vm((3,) + piece, BF),
            vm((2, 3) + piece, BF),
            vm((2, 4) + piece, BF),
            vm((2, 4) + piece, BF),
            vm((2, 4, 16, WIDTH), F32),
            vm((2, 4, 16, WIDTH), BF),
            vm((2, 4, 16, WIDTH), BF),
            vm((8, 16, 128), BF),
            vm((8, 16, 128), BF),
            vm((8, 16, 128), BF),
            vm((2, 2, 4, 4, 16, WIDTH), BF),
            vm((1,) + piece, F32),
            vm(piece, BF),
            dma((NSEND,)),
            dma((48,)),
            dma((4,)),
            dma((8 * NCH,)),
            dma((16 * NCH,)),
            dma((4,)),
            dma((4 * NCH,)),
            dma((32,)),
            dma((16,)),
            dma((16,)),
            dma((2,)),
            dma((2,)),
            dma((8,)),
            dma((8,)),
            dma((8,)),
            dma((8,)),
            dma((8,)),
            dma((8,)),
            dma((8,)),
            dma((17,)),
        ],
        compiler_params=pltpu.CompilerParams(collective_id=0, has_side_effects=True),
    )(block_index[0, 0], block_count, features, cotangent, w_first, w_second, block_values[0, 0])
    grads = grads.reshape(2, WIDTH, WIDTH).astype(F32)
    return out, grads[0], grads[1]


def solution(mesh):
    return jax.shard_map(
        local,
        mesh=mesh,
        in_specs=(
            P(("row", "col"), None),
            P(),
            P(),
            P("row", "col", None),
            P("row", "col"),
            P("row", "col", None, None, None),
            P(("row", "col"), None),
        ),
        out_specs=(P(("row", "col"), None), P(), P()),
        check_vma=False,
    )
```
